128 devices in a mesh: grp: 8 (over y, core), lane: 16 (over x, z).
Axes of the slice: x: 4, y: 4, z: 4, core: 2. Of those that a mesh axis runs over, the one named last changes fastest.
Arguments:
- fine_in: bfloat16 [2, 2048, 16, 256], P(None, ('grp', 'lane')), may hold values from -6 to 6
- counts: int32 [2, 128], P(None, ('grp', 'lane')), may hold values from 1 to 15, as said below
- neighbour_refs: int32 [2, 2048, 16], P(None, ('grp', 'lane')), may hold values from 0 to 271, as said below
- offset_codes: int32 [2, 2048, 16], P(None, ('grp', 'lane')), may hold values from 0 to 26, as said below
- neighbour_mask: int32 [2, 2048, 16], P(None, ('grp', 'lane')), may hold values 0 or 1
- send_slots: int32 [2, 128, 256], P(None, ('grp', 'lane')), may hold values from 0 to 14, as said below
- parent_of: int32 [2048], P(('grp', 'lane')), may hold values from -1 to 15, as said below
- child_code: int32 [2048], P(('grp', 'lane')), may hold values from 0 to 7, as said below
- coarse_refs: int32 [128, 16], P(('grp', 'lane')), may hold values from 0 to 127
- coarse_codes: int32 [128, 16], P(('grp', 'lane')), may hold values from 0 to 26, as said below
- coarse_mask: int32 [128, 16], P(('grp', 'lane')), may hold values 0 or 1
- ops_x: bfloat16 [3, 4, 3, 16, 16], replicated, may hold values from -0.75 to 0.75
- ops_y: bfloat16 [3, 4, 3, 16, 16], replicated, may hold values from -0.75 to 0.75
- ops_z: bfloat16 [3, 4, 3, 16, 16], replicated, may hold values from -0.75 to 0.75
- filters: bfloat16 [2, 16, 16], replicated, may hold values from -1.5 to 1.5
Outputs:
- fine_out: bfloat16 [2, 2048, 16, 256], P(None, ('grp', 'lane'))
- coarse_out: bfloat16 [128, 16, 256], P(('grp', 'lane'))
The draws below stay inside these ranges and needn't reach their ends.
Inputs may be any that keep to these rules, and one draw needn't show every extreme that they name: The counts of the devices of one grp index add up to 128 on level 1. send_slots[l, q, r * 2 + c] is a live slot of device q on level l. `neighbour_refs`: A value below 16 is a live slot of the block's own device; a larger one is 16 + q * 2 + c, entry c of what device q sends to the block's device. `offset_codes`: the codes of one block are distinct. `coarse_codes`: the codes of one coarse block are distinct. `parent_of`: -1 exactly on slots that are not live on level 1; every coarse block of a subtree has 8 live children there, one of each child code. `child_code`: 0 on slots that are not live.
All inputs are finite; a program needn't handle non-finite values. No bound on the sum of `neighbour_mask` or of `coarse_mask` on one device may be relied on, other than what follows from the above.
Results may differ from the reference program's by a relative error of at most 0.0088.
Values may be sent and summed in bfloat16 or wider, within the bound.
No kernel may reach another device: no remote copies, remote signals or barrier semaphores. Data moves between devices by JAX's collectives and lax.ppermute only.
A program may use at most 256 MiB of HBM per device.

```python
import jax
import jax.numpy as jnp
from jax import lax

K = 16
TERMS = 4
NB = 16
PAR_LANE = 1
CAP = 2
SLOT = 16
BLOCKS = 2048
PAR_GRP = 16
PAR = 128
N_GRP = 8
N_LANE = 16
DEVICES = 128


def live_counts(key, level_index):
    pair_count = DEVICES // 2
    middle = 8 * PAR_LANE
    spread = jax.random.randint(jax.random.fold_in(key, 101 + level_index), (pair_count,), 0, middle)
    spread = jnp.where(jnp.arange(pair_count, dtype=jnp.int32) == 0, middle - 1, spread)
    return jnp.stack([middle + spread, middle - spread], axis=1).reshape(DEVICES).astype(jnp.int32)


def distinct_codes(key, row_total):
    scores = jax.random.randint(key, (row_total, 27), 0, 1 << 20) * 32 + jnp.arange(27, dtype=jnp.int32)[None, :]
    ordering = jnp.argsort(scores, axis=1)
    return ordering[:, :NB].astype(jnp.int32)


def neighbour_table(key, level_index):
    counts_level = live_counts(key, level_index)
    slot_ids = jnp.arange(BLOCKS, dtype=jnp.int32)
    local_count = counts_level[slot_ids // SLOT][:, None]
    keys = jax.random.split(jax.random.fold_in(key, 201 + level_index), 3)
    own_slot = jax.random.randint(keys[0], (BLOCKS, NB), 0, 1 << 20) % local_count
    far_slot = SLOT + jax.random.randint(keys[1], (BLOCKS, NB), 0, DEVICES * CAP)
    choose_far = jax.random.randint(keys[2], (BLOCKS, NB), 0, 2)
    return jnp.where(choose_far == 1, far_slot, own_slot).astype(jnp.int32)


def send_table(key, level_index):
    counts_level = live_counts(key, level_index)
    raw_slots = jax.random.randint(jax.random.fold_in(key, 601 + level_index), (DEVICES, DEVICES * CAP), 0, 1 << 20)
    return (raw_slots % counts_level[:, None]).astype(jnp.int32)


def family(key):
    counts_one = live_counts(key, 1)
    slot_ids = jnp.arange(BLOCKS, dtype=jnp.int32)
    live_mask = slot_ids % SLOT < counts_one[slot_ids // SLOT]
    flags = live_mask.astype(jnp.int32).reshape(N_GRP, SLOT * N_LANE)
    ranks = jnp.cumsum(flags, axis=1) - 1
    children = 8 * PAR_LANE * N_LANE
    scores = jax.random.randint(jax.random.fold_in(key, 301), (N_GRP, children), 0, 1 << 18) * 4096 + jnp.arange(children, dtype=jnp.int32)[None, :]
    ordering = jnp.argsort(scores, axis=1).astype(jnp.int32)
    position = jnp.take_along_axis(ordering, jnp.maximum(ranks, 0), axis=1).reshape(BLOCKS)
    parent = jnp.where(live_mask, position // 8, -1).astype(jnp.int32)
    code_value = jnp.where(live_mask, position % 8, 0).astype(jnp.int32)
    return (parent, code_value)


def draw_counts(key, part):
    return jnp.stack([live_counts(key, 0), live_counts(key, 1)])


def draw_neighbour_refs(key, part):
    return jnp.stack([neighbour_table(key, 0), neighbour_table(key, 1)])


def draw_offset_codes(key, part):
    return jnp.stack([distinct_codes(jax.random.fold_in(key, 401), BLOCKS), distinct_codes(jax.random.fold_in(key, 402), BLOCKS)])


def draw_send_slots(key, part):
    return jnp.stack([send_table(key, 0), send_table(key, 1)])


def draw_parent_of(key, part):
    return family(key)[0]


def draw_child_code(key, part):
    return family(key)[1]


def draw_coarse_codes(key, part):
    return distinct_codes(jax.random.fold_in(key, 501), PAR)


def place_ends(values, key, least, largest):
    place = [jax.random.randint(jax.random.fold_in(key, axis), (), 0, length) for axis, length in enumerate(values.shape)]
    main_axis = values.shape.index(max(values.shape))
    next_to = place[:main_axis] + [(place[main_axis] + 1) % values.shape[main_axis]] + place[main_axis + 1:]
    return values.at[tuple(place)].set(least).at[tuple(next_to)].set(largest)


def steps_of(own_key, extent, cuts, low, high):
    def one(dim, parts):
        steps = jax.random.uniform(jax.random.fold_in(jax.random.fold_in(own_key, 6), dim), (parts,), jnp.float32, low / len(cuts), high / len(cuts))
        return jnp.repeat(jnp.exp(steps), extent[dim] // parts).reshape((-1,) + (1,) * (len(extent) - dim - 1))

    factor_of = one(*cuts[0])
    for cut in cuts[1:]:
        factor_of = factor_of * one(*cut)
    return factor_of


def bell_draw(stream_key, extent, scale, most, shards=(), kind=jnp.bfloat16):
    loudness = steps_of(stream_key, extent, shards, -0.22, 0.18) if shards else 1.0
    array = jax.random.normal(stream_key, extent, jnp.float32) * scale * loudness
    return jnp.minimum(jnp.maximum(array, -most), most).astype(kind)


def setup_inputs(seed: int = 0) -> dict:
    key_of = jax.random.split(jax.random.key(seed), 16)
    return {
        "fine_in": bell_draw(key_of[0], (2, BLOCKS, K, K * K), 1.0, 6.0, ((1, 128),)),
        "counts": draw_counts(jax.random.fold_in(key_of[15], 71), 0),
        "neighbour_refs": draw_neighbour_refs(jax.random.fold_in(key_of[15], 71), 0),
        "offset_codes": draw_offset_codes(jax.random.fold_in(key_of[15], 71), 0),
        "neighbour_mask": place_ends((jax.random.randint(key_of[4], (2, BLOCKS, NB), 0, 4) < 3).astype(jnp.int32), jax.random.fold_in(key_of[4], 1), 0, 1),
        "send_slots": draw_send_slots(jax.random.fold_in(key_of[15], 71), 0),
        "parent_of": draw_parent_of(jax.random.fold_in(key_of[15], 71), 0),
        "child_code": draw_child_code(jax.random.fold_in(key_of[15], 71), 0),
        "coarse_refs": place_ends(jax.random.randint(key_of[8], (PAR, NB), 0, PAR), jax.random.fold_in(key_of[8], 1), 0, PAR - 1).astype(jnp.int32),
        "coarse_codes": draw_coarse_codes(jax.random.fold_in(key_of[15], 71), 0),
        "coarse_mask": place_ends((jax.random.randint(key_of[10], (PAR, NB), 0, 4) < 3).astype(jnp.int32), jax.random.fold_in(key_of[10], 1), 0, 1),
        "ops_x": bell_draw(key_of[11], (3, TERMS, 3, K, K), (4 * K) ** -0.5, 0.75),
        "ops_y": bell_draw(key_of[12], (3, TERMS, 3, K, K), (4 * K) ** -0.5, 0.75),
        "ops_z": bell_draw(key_of[13], (3, TERMS, 3, K, K), (4 * K) ** -0.5, 0.75),
        "filters": bell_draw(key_of[14], (2, K, K), K ** -0.5, 1.5),
    }


offset_total = 27


def kron_tables(left_ops, right_ops):
    first = left_ops.astype(jnp.float32)[:, :, None, :, None, :, None]
    second = right_ops.astype(jnp.float32)[:, None, :, None, :, None, :]
    order_size = left_ops.shape[-1]
    product_full = first * second
    return product_full.reshape(-1, order_size * order_size, order_size * order_size).astype(jnp.bfloat16)


def apply_blocks(source_blocks, offset_codes, neighbour_mask, row_ops, tables):
    row_count = source_blocks.shape[0]
    order_size = source_blocks.shape[2]
    select = ((offset_codes[:, :, None] == jnp.arange(offset_total, dtype=jnp.int32)[None, None, :]) & (neighbour_mask[:, :, None] == 1)).astype(jnp.float32)
    grouped = jnp.einsum("bjc,bjxy->bcxy", select, source_blocks.astype(jnp.float32)).astype(jnp.bfloat16)
    grouped = grouped.reshape(row_count, 3, 9, order_size, order_size * order_size)
    spread = jnp.einsum("mapq,bacqr->bmcpr", row_ops.astype(jnp.float32), grouped.astype(jnp.float32)).astype(jnp.bfloat16)
    spread = spread.reshape(row_count, -1, order_size, order_size * order_size)
    return jnp.einsum("bcpr,csr->bps", spread.astype(jnp.float32), tables.astype(jnp.float32))


def corner_sum(lifted_rows, filter_tables, corner, transpose):
    block_count = corner.shape[0]
    running = jnp.zeros(lifted_rows.shape, jnp.float32)
    for corner_index in range(4):
        filter_table = filter_tables[corner_index].T if transpose else filter_tables[corner_index]
        product = jnp.dot(lifted_rows, filter_table, preferred_element_type=jnp.float32)
        chosen = jnp.repeat(corner == corner_index, lifted_rows.shape[0] // block_count)[:, None]
        running = running + jnp.where(chosen, product, jnp.zeros_like(product))
    return running.reshape(block_count, -1, lifted_rows.shape[1])


def source_index(neighbour_refs, send_slots):
    owner = (jnp.arange(neighbour_refs.shape[0], dtype=jnp.int32) // SLOT)[:, None]
    far_entry = jnp.maximum(neighbour_refs - SLOT, 0)
    peer_index = far_entry // CAP
    sent_slot = send_slots[peer_index, owner * CAP + far_entry % CAP]
    return jnp.where(neighbour_refs < SLOT, owner * SLOT + neighbour_refs, peer_index * SLOT + sent_slot).astype(jnp.int32)


def fine_level(blocks, counts, neighbour_refs, offset_codes, neighbour_mask, send_slots, row_ops, tables):
    slot_ids = jnp.arange(blocks.shape[0], dtype=jnp.int32)
    live_mask = (slot_ids % SLOT) < counts[slot_ids // SLOT]
    masked = jnp.where(live_mask[:, None, None], blocks, jnp.zeros_like(blocks))
    anchor = source_index(neighbour_refs, send_slots)

    def one_device(pieces):
        anchor_rows, code_rows, mask_rows = pieces
        return apply_blocks(masked[anchor_rows], code_rows, mask_rows, row_ops, tables)

    def shaped(values):
        return values.reshape(DEVICES, SLOT, -1)

    result = lax.map(one_device, (shaped(anchor), shaped(offset_codes), shaped(neighbour_mask)))
    result = result.reshape(blocks.shape[0], blocks.shape[1], blocks.shape[2])
    return jnp.where(live_mask[:, None, None], result, jnp.zeros_like(result)), live_mask, masked


def reference(fine_in, counts, neighbour_refs, offset_codes, neighbour_mask, send_slots, parent_of, child_code, coarse_refs, coarse_codes, coarse_mask, ops_x, ops_y, ops_z, filters):
    fine_terms = []
    masked_levels = []
    live_levels = []
    for level_index in range(2):
        tables = kron_tables(ops_y[level_index], ops_z[level_index])
        result, live_mask, masked = fine_level(fine_in[level_index], counts[level_index], neighbour_refs[level_index], offset_codes[level_index], neighbour_mask[level_index], send_slots[level_index], ops_x[level_index], tables)
        fine_terms.append(result)
        masked_levels.append(masked)
        live_levels.append(live_mask)
    filter_tables = kron_tables(filters[None], filters[None])
    upper_bit = child_code // 4
    corner = child_code % 4
    flat = masked_levels[1].astype(jnp.float32)
    lower_lift = jnp.einsum("pq,bqr->bpr", filters[0].astype(jnp.float32), flat)
    upper_lift = jnp.einsum("pq,bqr->bpr", filters[1].astype(jnp.float32), flat)
    lifted = jnp.where((upper_bit == 0)[:, None, None], lower_lift, upper_lift).astype(jnp.bfloat16)
    sibling_term = corner_sum(lifted.reshape(-1, K * K), filter_tables, corner, True)
    slot_ids = jnp.arange(parent_of.shape[0], dtype=jnp.int32)
    parent_global = (slot_ids // (SLOT * N_LANE)) * PAR_GRP + jnp.maximum(parent_of, 0)
    coarse_in = jax.ops.segment_sum(sibling_term, parent_global, num_segments=PAR).astype(jnp.bfloat16)
    coarse_tables = kron_tables(ops_y[2], ops_z[2])

    def one_coarse(pieces):
        ref_rows, code_rows, mask_rows = pieces
        return apply_blocks(coarse_in[ref_rows], code_rows, mask_rows, ops_x[2], coarse_tables)

    coarse_full = lax.map(one_coarse, (coarse_refs.reshape(DEVICES, PAR_LANE, -1), coarse_codes.reshape(DEVICES, PAR_LANE, -1), coarse_mask.reshape(DEVICES, PAR_LANE, -1)))
    coarse_out = coarse_full.reshape(PAR, K, K * K).astype(jnp.bfloat16)
    picked = jnp.where(live_levels[1][:, None, None], coarse_out[parent_global], jnp.zeros((parent_of.shape[0], K, K * K), jnp.bfloat16))
    flat_picked = picked.astype(jnp.float32)
    lower_drop = jnp.einsum("qp,bqr->bpr", filters[0].astype(jnp.float32), flat_picked)
    upper_drop = jnp.einsum("qp,bqr->bpr", filters[1].astype(jnp.float32), flat_picked)
    lowered = jnp.where((upper_bit == 0)[:, None, None], lower_drop, upper_drop).astype(jnp.bfloat16)
    correction = corner_sum(lowered.reshape(-1, K * K), filter_tables, corner, False)
    fine_one = fine_terms[1] + correction
    fine_out = jnp.stack([fine_terms[0], fine_one]).astype(jnp.bfloat16)
    return fine_out, coarse_out
```

```python
import jax
import jax.numpy as jnp
from jax import lax
from jax.experimental import pallas as pl
from jax.experimental.pallas import tpu as pltpu
from jax.sharding import PartitionSpec as P

K = 16
KK = K * K
TERMS = 4
SLOT = 16
CAP = 2
CODES = 27
BF = jnp.bfloat16
F32 = jnp.float32
AXES = ("grp", "lane")


def iota(shape, dim):
    return lax.broadcasted_iota(jnp.int32, shape, dim)


def spreads():
    row, col = iota((K, KK), 0), iota((K, KK), 1)
    return (col // K == row).astype(BF), (col % K == row).astype(BF)


def dot(a, b):
    return jnp.dot(a, b, preferred_element_type=F32)


def corner_tables(rep, tile):
    rows = []
    for cy in range(2):
        for cz in range(2):
            for p in range(K):
                rows.append((rep[cy][p : p + 1, :] * tile[cz]).astype(BF))
    return jnp.concatenate(rows, axis=0)


def corner_spread(blocks, code_ref):
    columns = []
    for corner in range(4):
        rows = []
        for b in range(SLOT):
            part = blocks[b * K : (b + 1) * K, :]
            rows.append(jnp.where(code_ref[b] % 4 == corner, part, jnp.zeros_like(part)))
        columns.append(jnp.concatenate(rows, axis=0))
    return jnp.concatenate(columns, axis=1)


def lift_kernel(parent_ref, code_ref, x_ref, filt_ref, filt_t_ref, info_ref, out_ref, acc_ref):
    repeat, tiled = spreads()
    tile_n = [dot(filt_ref[c], tiled) for c in range(2)]
    rep_t = [dot(filt_t_ref[c], repeat) for c in range(2)]
    tile_t = [dot(filt_t_ref[c], tiled) for c in range(2)]
    lane_block = iota((K, KK), 1) // K
    rows = []
    for b in range(SLOT):
        chosen = jnp.where(code_ref[b] // 4 == 1, tile_n[1], tile_n[0])
        rows.append(jnp.where(lane_block == b, chosen, 0.0).astype(BF))
    lifted = dot(jnp.concatenate(rows, axis=0), x_ref[0].reshape(SLOT * K, KK)).astype(BF)
    moved = dot(corner_spread(lifted, code_ref), corner_tables(rep_t, tile_t))
    acc_ref[...] = jnp.zeros_like(acc_ref)
    for b in range(SLOT):
        parent = parent_ref[b]
        target = jnp.where(parent < 0, SLOT, parent)
        acc_ref[target] = acc_ref[target] + moved[b * K : (b + 1) * K, :]
    for t in range(SLOT):
        out_ref[t, 0:K, :] = acc_ref[t].astype(BF)
        out_ref[t, K : K + 8, :] = info_ref[...]


def gather_kernel(slots_ref, fine_ref, out_ref):
    step = pl.program_id(0)
    for r in range(16):
        for level in range(2):
            for c in range(CAP):
                slot = slots_ref[level * 256 + (step * 16 + r) * CAP + c]
                out_ref[r, level * CAP + c] = fine_ref[level, slot]


def place_kernel(recv_ref, send_in_ref, send_ref, copies_ref, sem):
    total = recv_ref[0, 0:K, :].astype(F32)
    for lane in range(1, 16):
        total = total + recv_ref[lane, 0:K, :].astype(F32)
    mine = total.astype(BF)
    for r in range(128):
        copies_ref[r] = mine
    copy = pltpu.make_async_copy(copies_ref, send_ref.at[:, 4], sem)
    copy.start()
    copy.wait()


def tail_kernel(
    idx_ref,
    parent_ref,
    code_ref,
    place_ref,
    arrived_ref,
    fine_ref,
    xbd_ref,
    yw_ref,
    zw_ref,
    filt_ref,
    filt_t_ref,
    fine_out_ref,
    coarse_out_ref,
    pool_ref,
    spread_ref,
    table_ref,
    acc_ref,
    coarse_ref,
    sems,
):
    copies = [
        pltpu.make_async_copy(fine_ref.at[0], pool_ref.at[128:144, 0], sems.at[0]),
        pltpu.make_async_copy(arrived_ref.at[:, 0:2], pool_ref.at[0:128, 0:2], sems.at[1]),
        pltpu.make_async_copy(fine_ref.at[1], pool_ref.at[128:144, 1], sems.at[2]),
        pltpu.make_async_copy(arrived_ref.at[:, 2:4], pool_ref.at[0:128, 2:4], sems.at[3]),
        pltpu.make_async_copy(arrived_ref.at[:, 4], pool_ref.at[0:128, 4], sems.at[4]),
    ]
    for copy in copies:
        copy.start()
    pool_ref[144, 0] = jnp.zeros((K, KK), BF)

    def apply_level(level):
        xbd = xbd_ref[level]
        acc_ref[...] = jnp.zeros_like(acc_ref)

        def step(cyz, carry):
            cy = cyz // 3
            cz = cyz % 3
            for g4 in range(4):
                parts = []
                for b4 in range(4):
                    for cx in range(3):
                        v = idx_ref[(level * SLOT + g4 * 4 + b4) * CODES + 9 * cx + cyz]
                        parts.append(pool_ref[v // 8, v % 8])
                spread = dot(xbd, jnp.concatenate(parts, axis=0)).astype(BF)
                for m in range(TERMS):
                    spread_ref[g4 * 64 : (g4 + 1) * 64, m * KK : (m + 1) * KK] = spread[
                        m * 64 : (m + 1) * 64, :
                    ]
            for m in range(TERMS):
                zpart = zw_ref[level, m * 3 + cz]
                ypart = yw_ref[level, m * 3 + cy]
                for r in range(K):
                    table_ref[m * KK + r * K : m * KK + (r + 1) * K, :] = (
                        ypart[r : r + 1, :] * zpart
                    ).astype(BF)
            acc_ref[...] += dot(spread_ref[...], table_ref[...])
            return carry

        lax.fori_loop(0, 9, step, 0)

    for level in range(2):
        copies[2 * level].wait()
        copies[2 * level + 1].wait()
        apply_level(level)
        for b in range(SLOT):
            live = b < place_ref[level]
            rows = acc_ref[b * K : (b + 1) * K, :]
            rows = jnp.where(live, rows, 0.0)
            if level == 0:
                fine_out_ref[0, b] = rows.astype(BF)
            else:
                coarse_ref[1, b] = rows
    copies[4].wait()
    apply_level(2)
    for t in range(SLOT):
        coarse_ref[0, t] = acc_ref[t * K : (t + 1) * K, :]
    coarse_out_ref[0] = coarse_ref[0, place_ref[2]].astype(BF)

    repeat, tiled = spreads()
    rep_n = [dot(filt_ref[c], repeat) for c in range(2)]
    tile_n = [dot(filt_ref[c], tiled) for c in range(2)]
    tile_t = [dot(filt_t_ref[c], tiled) for c in range(2)]
    lane_block = iota((K, KK), 1) // K
    rows = []
    for b in range(SLOT):
        chosen = jnp.where(code_ref[b] // 4 == 1, tile_t[1], tile_t[0])
        rows.append(jnp.where(lane_block == parent_ref[b], chosen, 0.0).astype(BF))
    lowered = dot(jnp.concatenate(rows, axis=0), acc_ref[...].astype(BF)).astype(BF)
    correction = dot(corner_spread(lowered, code_ref), corner_tables(rep_n, tile_n))
    for b in range(SLOT):
        fine_out_ref[1, b] = (coarse_ref[1, b] + correction[b * K : (b + 1) * K, :]).astype(BF)


def smem():
    return pl.BlockSpec(memory_space=pltpu.SMEM)


def vmem():
    return pl.BlockSpec(memory_space=pltpu.VMEM)


def anywhere():
    return pl.BlockSpec(memory_space=pl.ANY)


def code_index(codes, mask, places, empty):
    hits = (codes[:, None, :] == jnp.arange(CODES, dtype=jnp.int32)[None, :, None]) & (
        mask[:, None, :] == 1
    )
    return empty + jnp.sum(jnp.where(hits, places[:, None, :] - empty, 0), axis=2)


def body(
    fine_in,
    counts,
    neighbour_refs,
    offset_codes,
    neighbour_mask,
    send_slots,
    parent_of,
    child_code,
    coarse_refs,
    coarse_codes,
    coarse_mask,
    ops_x,
    ops_y,
    ops_z,
    filters,
):
    filters_t = jnp.swapaxes(filters, 1, 2)
    info = jnp.concatenate([coarse_refs, coarse_codes, coarse_mask], axis=0).astype(BF)
    info = jnp.pad(info, ((0, 5), (0, KK - 16)))
    partial = pl.pallas_call(
        lift_kernel,
        grid=(1,),
        in_specs=[
            smem(),
            smem(),
            pl.BlockSpec((1, SLOT, K, KK), lambda i: (1, 0, 0, 0)),
            vmem(),
            vmem(),
            vmem(),
        ],
        out_specs=vmem(),
        out_shape=jax.ShapeDtypeStruct((16, K + 8, KK), BF),
        scratch_shapes=[pltpu.VMEM((SLOT + 1, K, KK), F32)],
        name="lift",
    )(parent_of, child_code, fine_in, filters, filters_t, info)
    recv = lax.all_to_all(partial, "lane", split_axis=0, concat_axis=0, tiled=True)

    send = pl.pallas_call(
        gather_kernel,
        grid=(8,),
        in_specs=[smem(), vmem()],
        out_specs=pl.BlockSpec((16, 5, K, KK), lambda i: (i, 0, 0, 0)),
        out_shape=jax.ShapeDtypeStruct((128, 5, K, KK), BF),
        name="gather",
        cost_estimate=pl.CostEstimate(flops=1000, bytes_accessed=9_000_000, transcendentals=0),
    )(send_slots.reshape(512), fine_in)
    send = pl.pallas_call(
        place_kernel,
        in_specs=[vmem(), anywhere()],
        out_specs=anywhere(),
        out_shape=jax.ShapeDtypeStruct((128, 5, K, KK), BF),
        scratch_shapes=[pltpu.VMEM((128, K, KK), BF), pltpu.SemaphoreType.DMA],
        input_output_aliases={1: 0},
        name="place",
    )(recv, send)
    arrived = lax.all_to_all(send, AXES, split_axis=0, concat_axis=0, tiled=True)

    repeat, tiled = spreads()
    yw = jnp.einsum("lmcpr,pk->lmcrk", ops_y, repeat, preferred_element_type=F32)
    zw = jnp.einsum("lmcqs,qk->lmcsk", ops_z, tiled, preferred_element_type=F32)
    yw = yw.reshape(3, 12, K, KK)
    zw = zw.reshape(3, 12, K, KK)
    xm = jnp.transpose(ops_x, (0, 1, 3, 2, 4)).reshape(3, 64, 48)
    row, col = iota((256, 64), 0), iota((256, 64), 1)
    grow = ((row // 64 == col // 16) & (row % 16 == col % 16)).astype(BF)
    row, col = iota((48, 192), 0), iota((48, 192), 1)
    wide = (col % 48 == row).astype(BF)
    row, col = iota((256, 192), 0), iota((256, 192), 1)
    own = (row // 16) % 4 == col // 48
    xbd = jnp.einsum("ij,ljk->lik", grow, xm)
    xbd = jnp.einsum("lik,kn->lin", xbd, wide)
    xbd = jnp.where(own[None], xbd, jnp.zeros_like(xbd))

    empty = 144 * 8
    tables = []
    for level in range(2):
        refs = neighbour_refs[level]
        far = refs - SLOT
        places = jnp.where(
            refs < SLOT, (128 + refs) * 8 + level, (far // CAP) * 8 + CAP * level + far % CAP
        )
        tables.append(code_index(offset_codes[level], neighbour_mask[level], places, empty))
    lists = recv[:, K : K + 3, 0:16].astype(jnp.int32)
    tables.append(code_index(lists[:, 1], lists[:, 2], lists[:, 0] * 8 + 4, empty))
    idx = jnp.concatenate([t.reshape(-1) for t in tables])
    place = jnp.concatenate(
        [counts[:, 0], lax.axis_index("lane").astype(jnp.int32).reshape(1)]
    )

    fine_out, coarse_out = pl.pallas_call(
        tail_kernel,
        in_specs=[smem()] * 4 + [anywhere()] * 2 + [vmem()] * 5,
        out_specs=[vmem(), vmem()],
        out_shape=[
            jax.ShapeDtypeStruct((2, SLOT, K, KK), BF),
            jax.ShapeDtypeStruct((1, K, KK), BF),
        ],
        scratch_shapes=[
            pltpu.VMEM((145, 5, K, KK), BF),
            pltpu.VMEM((KK, TERMS * KK), BF),
            pltpu.VMEM((TERMS * KK, KK), BF),
            pltpu.VMEM((KK, KK), F32),
            pltpu.VMEM((2, SLOT, K, KK), F32),
            pltpu.SemaphoreType.DMA((5,)),
        ],
        name="tail",
    )(
        idx,
        parent_of,
        child_code,
        place,
        arrived,
        fine_in,
        xbd,
        yw,
        zw,
        filters,
        filters_t,
    )
    return fine_out, coarse_out


def solution(mesh):
    blocks = P(None, AXES, None, None)
    table = P(None, AXES, None)
    in_specs = (
        blocks,
        P(None, AXES),
        table,
        table,
        table,
        table,
        P(AXES),
        P(AXES),
        P(AXES, None),
        P(AXES, None),
        P(AXES, None),
        P(),
        P(),
        P(),
        P(),
    )
    out_specs = (blocks, P(AXES, None, None))
    return jax.shard_map(body, mesh=mesh, in_specs=in_specs, out_specs=out_specs, check_vma=False)
```

```python
import jax
import jax.numpy as jnp
from jax import lax
from jax.experimental import pallas as pl
from jax.experimental.pallas import tpu as pltpu
from jax.sharding import PartitionSpec as P

K = 16
KK = K * K
TERMS = 4
SLOT = 16
CAP = 2
CODES = 27
BF = jnp.bfloat16
F32 = jnp.float32
AXES = ("grp", "lane")


def iota(shape, dim):
    return lax.broadcasted_iota(jnp.int32, shape, dim)


def spreads():
    row, col = iota((K, KK), 0), iota((K, KK), 1)
    return (col // K == row).astype(BF), (col % K == row).astype(BF)


def dot(a, b):
    return jnp.dot(a, b, preferred_element_type=F32)


def corner_tables(rep, tile):
    rows = []
    for cy in range(2):
        for cz in range(2):
            for p in range(K):
                rows.append((rep[cy][p : p + 1, :] * tile[cz]).astype(BF))
    return jnp.concatenate(rows, axis=0)


def corner_spread(blocks, code_ref):
    columns = []
    for corner in range(4):
        rows = []
        for b in range(SLOT):
            part = blocks[b * K : (b + 1) * K, :]
            rows.append(jnp.where(code_ref[b] % 4 == corner, part, jnp.zeros_like(part)))
        columns.append(jnp.concatenate(rows, axis=0))
    return jnp.concatenate(columns, axis=1)


def factors(filt_ref):
    repeat, tiled = spreads()
    flip = lambda f, e: lax.dot_general(f, e, (((0,), (0,)), ((), ())), preferred_element_type=F32)
    filts = [filt_ref[c] for c in range(2)]
    rep_n = [dot(f, repeat) for f in filts]
    tile_n = [dot(f, tiled) for f in filts]
    rep_t = [flip(f, repeat) for f in filts]
    tile_t = [flip(f, tiled) for f in filts]
    return rep_n, tile_n, rep_t, tile_t


def send_kernel(
    parent_ref,
    code_ref,
    slots_ref,
    grp_ref,
    fine_ref,
    filt_ref,
    refs_ref,
    codes_ref,
    mask_ref,
    send_ref,
    pack_ref,
    piece_ref,
    acc_ref,
    sems,
):
    copies = []
    for chunk in range(4):
        def fill(r, carry):
            for level in range(2):
                for c in range(CAP):
                    slot = slots_ref[level, 0, r * CAP + c]
                    at = 32 * (level * CAP + c)
                    block = fine_ref[level, slot]
                    pack_ref[r, at : at + 16, :] = block[:, 0:128]
                    pack_ref[r, at + 16 : at + 32, :] = block[:, 128:256]
            return carry

        lax.fori_loop(chunk * 32, chunk * 32 + 32, fill, 0, unroll=4)
        here = pl.ds(chunk * 32, 32)
        copies.append(
            pltpu.make_async_copy(
                pack_ref.at[here], send_ref.at[here, pl.ds(0, 128)], sems.at[chunk]
            )
        )
        copies[-1].start()

    _, tile_n, rep_t, tile_t = factors(filt_ref)
    lane_block = iota((K, KK), 1) // K
    rows = []
    for b in range(SLOT):
        chosen = jnp.where(code_ref[b] // 4 == 1, tile_n[1], tile_n[0])
        rows.append(jnp.where(lane_block == b, chosen, 0.0).astype(BF))
    lifted = dot(jnp.concatenate(rows, axis=0), fine_ref[1].reshape(SLOT * K, KK)).astype(BF)
    moved = dot(corner_spread(lifted, code_ref), corner_tables(rep_t, tile_t))
    parity = grp_ref[0] % 2
    info = jnp.concatenate([refs_ref[...], codes_ref[...]] + [mask_ref[...]] * 6, axis=0)
    wide = (iota((16, 128), 0) == iota((16, 128), 1)).astype(BF)
    info = dot(info.astype(F32).astype(BF), wide).astype(BF)
    for gp in range(4):
        for lane in range(16):
            piece_ref[(2 * gp + parity) * 16 + lane] = info
    acc_ref[...] = jnp.zeros_like(acc_ref)
    for b in range(SLOT):
        parent = parent_ref[b]
        target = jnp.where(parent < 0, SLOT, parent)
        acc_ref[target] = acc_ref[target] + moved[b * K : (b + 1) * K, :]
    for t in range(SLOT):
        for half in range(2):
            for top in range(2):
                tile = acc_ref[t, top * 8 : top * 8 + 8, half * 128 : half * 128 + 128].astype(BF)
                j = t * 4 + half * 2 + top
                piece_ref[(2 * (j // 16) + 1 - parity) * 16 + j % 16] = tile
    copies.append(
        pltpu.make_async_copy(piece_ref, send_ref.at[:, pl.ds(128, 8)], sems.at[4])
    )
    copies[-1].start()
    for copy in copies:
        copy.wait()


def place_kernel(grp_ref, arrived_ref, out_ref, info_ref, piece_ref, sem):
    parity = grp_ref[0] % 2
    copy = pltpu.make_async_copy(arrived_ref.at[:, :, :, pl.ds(128, 8)], piece_ref, sem)
    copy.start()
    copy.wait()
    sums = []
    for g in range(4):
        total = piece_ref[g, 1 - parity, 0].astype(F32)
        for lane in range(1, 16):
            total = total + piece_ref[g, 1 - parity, lane].astype(F32)
        sums.append(total)
    mine = jnp.concatenate(sums, axis=0).astype(BF)
    for r in range(128):
        out_ref[r] = mine
    info_ref[...] = piece_ref[grp_ref[0] // 2, parity]


def apply_level(level, blocks, place, xbd_ref, yw_ref, zw_ref, spread_ref, table_ref, acc_ref):
    xbd = xbd_ref[level]

    def prepare(cyz):
        cy, cz, slot = cyz // 3, cyz % 3, cyz % 2
        for g4 in range(4):
            parts = []
            for b4 in range(4):
                for cx in range(3):
                    at = pl.multiple_of(place(g4 * 4 + b4, 9 * cx + cyz), 32)
                    parts.append(
                        jnp.concatenate(
                            [blocks[pl.ds(at, 16), :], blocks[pl.ds(at + 16, 16), :]], axis=1
                        )
                    )
            spread = dot(xbd, jnp.concatenate(parts, axis=0)).astype(BF)
            for m in range(TERMS):
                spread_ref[slot, g4 * 64 : (g4 + 1) * 64, m * KK : (m + 1) * KK] = spread[
                    m * 64 : (m + 1) * 64, :
                ]
        for m in range(TERMS):
            zpart = zw_ref[level, m * 3 + cz]
            ypart = yw_ref[level, m * 3 + cy]
            for r in range(K):
                table_ref[slot, m * KK + r * K : m * KK + (r + 1) * K, :] = (
                    ypart[r : r + 1, :] * zpart
                ).astype(BF)

    prepare(0)
    for cyz in range(9):
        if cyz < 8:
            prepare(cyz + 1)
        term = dot(spread_ref[cyz % 2], table_ref[cyz % 2])
        acc_ref[...] = term if cyz == 0 else acc_ref[...] + term


def fine_kernel(
    idx_ref,
    counts_ref,
    arrived_ref,
    fine_ref,
    info_ref,
    xbd_ref,
    yw_ref,
    zw_ref,
    out_ref,
    one_ref,
    coarse_idx_ref,
    pool_ref,
    spread_ref,
    table_ref,
    acc_ref,
    sems,
):
    copies = []
    for level in range(2):
        part = pl.ds(level * 64, 64)
        copies.append(
            pltpu.make_async_copy(
                arrived_ref.at[:, part], pool_ref.at[pl.ds(0, 128), part], sems.at[level]
            )
        )
        copies[-1].start()
    for level in range(2):
        for b in range(SLOT):
            block = fine_ref[level, b]
            pool_ref[128 + b, level * 64 : level * 64 + 16, :] = block[:, 0:128]
            pool_ref[128 + b, level * 64 + 16 : level * 64 + 32, :] = block[:, 128:256]
    pool_ref[144, 0:32, :] = jnp.zeros((32, 128), BF)
    lists = info_ref[...].astype(F32)
    refs, codes, mask = (lists[:, i, :] for i in range(3))
    codes = jnp.where(mask == 1.0, codes, -1.0)
    offset = iota((16, 128), 1).astype(F32)
    place = jnp.full((16, 128), 128.0, F32)
    for j in range(16):
        place = jnp.where(codes[:, j : j + 1] == offset, refs[:, j : j + 1], place)
    coarse_idx_ref[...] = place.astype(jnp.int32) * 32

    blocks = pool_ref.reshape(145 * 128, 128)

    for level in range(2):
        copies[level].wait()
        apply_level(
            level,
            blocks,
            lambda b, code: idx_ref[(level * SLOT + b) * CODES + code],
            xbd_ref,
            yw_ref,
            zw_ref,
            spread_ref,
            table_ref,
            acc_ref,
        )
        for b in range(SLOT):
            rows = jnp.where(b < counts_ref[level, 0], acc_ref[b * K : (b + 1) * K, :], 0.0)
            if level == 0:
                out_ref[0, b] = rows.astype(BF)
            else:
                one_ref[b] = rows


def tail_kernel(
    idx_ref,
    parent_ref,
    code_ref,
    lane_ref,
    summed_ref,
    one_ref,
    xbd_ref,
    yw_ref,
    zw_ref,
    filt_ref,
    fine_in_ref,
    fine_out_ref,
    coarse_out_ref,
    pool_ref,
    spread_ref,
    table_ref,
    acc_ref,
    coarse_ref,
    result_ref,
    sems,
):
    copies = []
    for g in range(8):
        copies.append(
            pltpu.make_async_copy(
                summed_ref.at[:, 1 - g % 2, :, g // 2], pool_ref.at[g], sems.at[g]
            )
        )
        copies[-1].start()
    pool_ref[8, 0, 0:4] = jnp.zeros((4, 8, 128), BF)
    blocks = pool_ref.reshape(9 * 512, 128)
    for copy in copies:
        copy.wait()

    apply_level(
        2,
        blocks,
        lambda b, code: idx_ref[b, code],
        xbd_ref,
        yw_ref,
        zw_ref,
        spread_ref,
        table_ref,
        acc_ref,
    )
    for t in range(SLOT):
        coarse_ref[t] = acc_ref[t * K : (t + 1) * K, :]
    coarse_out_ref[0] = coarse_ref[lane_ref[0]].astype(BF)

    rep_n, tile_n, _, tile_t = factors(filt_ref)
    lane_block = iota((K, KK), 1) // K
    rows = []
    for b in range(SLOT):
        chosen = jnp.where(code_ref[b] // 4 == 1, tile_t[1], tile_t[0])
        rows.append(jnp.where(lane_block == parent_ref[b], chosen, 0.0).astype(BF))
    lowered = dot(jnp.concatenate(rows, axis=0), acc_ref[...].astype(BF)).astype(BF)
    correction = dot(corner_spread(lowered, code_ref), corner_tables(rep_n, tile_n))
    for b in range(SLOT):
        result_ref[b] = (one_ref[b] + correction[b * K : (b + 1) * K, :]).astype(BF)
    copy = pltpu.make_async_copy(result_ref, fine_out_ref.at[1], sems.at[8])
    copy.start()
    copy.wait()


def smem():
    return pl.BlockSpec(memory_space=pltpu.SMEM)


def vmem():
    return pl.BlockSpec(memory_space=pltpu.VMEM)


def anywhere():
    return pl.BlockSpec(memory_space=pl.ANY)


def code_index(codes, mask, places, empty):
    hits = (codes[:, None, :] == jnp.arange(CODES, dtype=jnp.int32)[None, :, None]) & (
        mask[:, None, :] == 1
    )
    return empty + jnp.sum(jnp.where(hits, places[:, None, :] - empty, 0), axis=2)


def body(
    fine_in,
    counts,
    neighbour_refs,
    offset_codes,
    neighbour_mask,
    send_slots,
    parent_of,
    child_code,
    coarse_refs,
    coarse_codes,
    coarse_mask,
    ops_x,
    ops_y,
    ops_z,
    filters,
):
    grp = lax.axis_index("grp").astype(jnp.int32).reshape(1)
    lane = lax.axis_index("lane").astype(jnp.int32).reshape(1)
    send = pl.pallas_call(
        send_kernel,
        in_specs=[smem()] * 4 + [vmem()] * 5,
        out_specs=anywhere(),
        out_shape=jax.ShapeDtypeStruct((128, 136, 128), BF),
        scratch_shapes=[
            pltpu.VMEM((128, 128, 128), BF),
            pltpu.VMEM((128, 8, 128), BF),
            pltpu.VMEM((SLOT + 1, K, KK), F32),
            pltpu.SemaphoreType.DMA((5,)),
        ],
        name="send",
    )(
        parent_of,
        child_code,
        send_slots,
        grp,
        fine_in,
        filters,
        coarse_refs,
        coarse_codes,
        coarse_mask,
    )
    arrived = lax.all_to_all(send, AXES, split_axis=0, concat_axis=0, tiled=True)

    summed, info = pl.pallas_call(
        place_kernel,
        in_specs=[smem(), anywhere()],
        out_specs=[vmem(), vmem()],
        out_shape=[
            jax.ShapeDtypeStruct((128, 32, 128), BF),
            jax.ShapeDtypeStruct((16, 8, 128), BF),
        ],
        scratch_shapes=[pltpu.VMEM((4, 2, 16, 8, 128), BF), pltpu.SemaphoreType.DMA],
        name="place",
    )(grp, arrived.reshape(4, 2, 16, 136, 128))
    summed = lax.all_to_all(summed, AXES, split_axis=0, concat_axis=0, tiled=True)

    repeat, tiled = spreads()
    yw = jnp.einsum("lmcpr,pk->lmcrk", ops_y, repeat, preferred_element_type=F32)
    zw = jnp.einsum("lmcqs,qk->lmcsk", ops_z, tiled, preferred_element_type=F32)
    yw = yw.reshape(3, 12, K, KK)
    zw = zw.reshape(3, 12, K, KK)
    xm = jnp.transpose(ops_x, (0, 1, 3, 2, 4)).reshape(3, 64, 48)
    row, col = iota((256, 64), 0), iota((256, 64), 1)
    grow = ((row // 64 == col // 16) & (row % 16 == col % 16)).astype(BF)
    row, col = iota((48, 192), 0), iota((48, 192), 1)
    wide = (col % 48 == row).astype(BF)
    row, col = iota((256, 192), 0), iota((256, 192), 1)
    own = (row // 16) % 4 == col // 48
    xbd = jnp.einsum("ij,ljk->lik", grow, xm)
    xbd = jnp.einsum("lik,kn->lin", xbd, wide)
    xbd = jnp.where(own[None], xbd, jnp.zeros_like(xbd))

    empty = 144 * 128
    tables = []
    for level in range(2):
        refs = neighbour_refs[level]
        far = refs - SLOT
        places = jnp.where(
            refs < SLOT,
            (128 + refs) * 128 + level * 64,
            (far // CAP) * 128 + level * 64 + (far % CAP) * 32,
        )
        tables.append(code_index(offset_codes[level], neighbour_mask[level], places, empty))
    idx = jnp.concatenate([t.reshape(-1) for t in tables])
    work = [
        pltpu.VMEM((2, KK, TERMS * KK), BF),
        pltpu.VMEM((2, TERMS * KK, KK), BF),
        pltpu.VMEM((KK, KK), F32),
    ]
    fine_out, one, coarse_idx = pl.pallas_call(
        fine_kernel,
        in_specs=[smem()] * 2 + [anywhere()] + [vmem()] * 5,
        out_specs=[pl.BlockSpec((1, SLOT, K, KK), lambda i: (0, 0, 0, 0)), vmem(), vmem()],
        out_shape=[
            jax.ShapeDtypeStruct((2, SLOT, K, KK), BF),
            jax.ShapeDtypeStruct((SLOT, K, KK), F32),
            jax.ShapeDtypeStruct((16, 128), jnp.int32),
        ],
        grid=(1,),
        scratch_shapes=[pltpu.VMEM((145, 128, 128), BF)]
        + work
        + [pltpu.SemaphoreType.DMA((2,))],
        name="fine",
        cost_estimate=pl.CostEstimate(
            flops=10_000_000_000, bytes_accessed=6_000_000, transcendentals=0
        ),
    )(idx, counts, arrived, fine_in, info, xbd, yw, zw)

    fine_out, coarse_out = pl.pallas_call(
        tail_kernel,
        in_specs=[smem()] * 4 + [anywhere()] + [vmem()] * 5 + [anywhere()],
        out_specs=[anywhere(), vmem()],
        out_shape=[
            jax.ShapeDtypeStruct((2, SLOT, K, KK), BF),
            jax.ShapeDtypeStruct((1, K, KK), BF),
        ],
        scratch_shapes=[pltpu.VMEM((9, 4, 16, 8, 128), BF)]
        + work
        + [
            pltpu.VMEM((SLOT, K, KK), F32),
            pltpu.VMEM((SLOT, K, KK), BF),
            pltpu.SemaphoreType.DMA((9,)),
        ],
        input_output_aliases={10: 0},
        name="tail",
    )(
        coarse_idx,
        parent_of,
        child_code,
        lane,
        summed.reshape(4, 2, 16, 4, 8, 128),
        one,
        xbd,
        yw,
        zw,
        filters,
        fine_out,
    )
    return fine_out, coarse_out


def solution(mesh):
    blocks = P(None, AXES, None, None)
    table = P(None, AXES, None)
    in_specs = (
        blocks,
        P(None, AXES),
        table,
        table,
        table,
        table,
        P(AXES),
        P(AXES),
        P(AXES, None),
        P(AXES, None),
        P(AXES, None),
        P(),
        P(),
        P(),
        P(),
    )
    out_specs = (blocks, P(AXES, None, None))
    return jax.shard_map(body, mesh=mesh, in_specs=in_specs, out_specs=out_specs, check_vma=False)
```

```python
import jax
import jax.numpy as jnp
from jax import lax
from jax.experimental import pallas as pl
from jax.experimental.pallas import tpu as pltpu
from jax.sharding import PartitionSpec as P

K = 16
KK = K * K
TERMS = 4
SLOT = 16
CAP = 2
CODES = 27
GROUP = 4
BF = jnp.bfloat16
F32 = jnp.float32
AXES = ("grp", "lane")


def iota(shape, dim):
    return lax.broadcasted_iota(jnp.int32, shape, dim)


def spreads():
    row, col = iota((K, KK), 0), iota((K, KK), 1)
    return (col // K == row).astype(BF), (col % K == row).astype(BF)


def dot(a, b):
    return jnp.dot(a, b, preferred_element_type=F32)


def corner_tables(rep, tile):
    rows = []
    for cy in range(2):
        for cz in range(2):
            for p in range(K):
                rows.append((rep[cy][p : p + 1, :] * tile[cz]).astype(BF))
    return jnp.concatenate(rows, axis=0)


def corner_spread(blocks, code_ref):
    columns = []
    for corner in range(4):
        rows = []
        for b in range(SLOT):
            part = blocks[b * K : (b + 1) * K, :]
            rows.append(jnp.where(code_ref[b] % 4 == corner, part, jnp.zeros_like(part)))
        columns.append(jnp.concatenate(rows, axis=0))
    return jnp.concatenate(columns, axis=1)


def factors(filt_ref):
    repeat, tiled = spreads()
    flip = lambda f, e: lax.dot_general(f, e, (((0,), (0,)), ((), ())), preferred_element_type=F32)
    filts = [filt_ref[c] for c in range(2)]
    rep_n = [dot(f, repeat) for f in filts]
    tile_n = [dot(f, tiled) for f in filts]
    rep_t = [flip(f, repeat) for f in filts]
    tile_t = [flip(f, tiled) for f in filts]
    return rep_n, tile_n, rep_t, tile_t


def send_kernel(
    parent_ref,
    code_ref,
    slots_ref,
    fine_ref,
    filt_ref,
    refs_ref,
    codes_ref,
    mask_ref,
    send_ref,
    pack_ref,
    piece_ref,
    acc_ref,
    sems,
):
    copies = []
    for chunk in range(8):

        def fill(r, carry):
            for level in range(2):
                for c in range(CAP):
                    slot = slots_ref[level, 0, r * CAP + c]
                    at = 32 * (level * CAP + c)
                    block = fine_ref[level, slot]
                    pack_ref[r, at : at + 16, :] = block[:, 0:128]
                    pack_ref[r, at + 16 : at + 32, :] = block[:, 128:256]
            return carry

        lax.fori_loop(chunk * 16, chunk * 16 + 16, fill, 0, unroll=4)
        here = pl.ds(chunk * 16, 16)
        copies.append(
            pltpu.make_async_copy(
                pack_ref.at[here], send_ref.at[here, pl.ds(0, 128)], sems.at[chunk]
            )
        )
        copies[-1].start()

    _, tile_n, rep_t, tile_t = factors(filt_ref)
    lane_block = iota((K, KK), 1) // K
    rows = []
    for b in range(SLOT):
        chosen = jnp.where(code_ref[b] // 4 == 1, tile_n[1], tile_n[0])
        rows.append(jnp.where(lane_block == b, chosen, 0.0).astype(BF))
    lifted = dot(jnp.concatenate(rows, axis=0), fine_ref[1].reshape(SLOT * K, KK)).astype(BF)
    moved = dot(corner_spread(lifted, code_ref), corner_tables(rep_t, tile_t))
    parity = lax.axis_index("grp") % 2
    info = jnp.concatenate([refs_ref[...], codes_ref[...]] + [mask_ref[...]] * 6, axis=0)
    wide = (iota((16, 128), 0) == iota((16, 128), 1)).astype(BF)
    info = dot(info.astype(F32).astype(BF), wide).astype(BF)
    for gp in range(4):
        for lane in range(16):
            piece_ref[(2 * gp + parity) * 16 + lane] = info
    acc_ref[...] = jnp.zeros_like(acc_ref)
    for b in range(SLOT):
        parent = parent_ref[b]
        target = jnp.where(parent < 0, SLOT, parent)
        acc_ref[target] = acc_ref[target] + moved[b * K : (b + 1) * K, :]
    for t in range(SLOT):
        for half in range(2):
            for top in range(2):
                tile = acc_ref[t, top * 8 : top * 8 + 8, half * 128 : half * 128 + 128].astype(BF)
                j = t * 4 + half * 2 + top
                piece_ref[(2 * (j % 4) + 1 - parity) * 16 + j // 4] = tile
    copies.append(
        pltpu.make_async_copy(piece_ref, send_ref.at[:, pl.ds(128, 8)], sems.at[8])
    )
    copies[-1].start()
    for copy in copies:
        copy.wait()


def place_kernel(arrived_ref, out_ref, info_ref, piece_ref, sem):
    grp = lax.axis_index("grp")
    parity = grp % 2
    copy = pltpu.make_async_copy(arrived_ref.at[:, :, :, pl.ds(128, 8)], piece_ref, sem)
    copy.start()
    copy.wait()
    sums = []
    for g in range(4):
        total = piece_ref[g, 1 - parity, 0].astype(F32)
        for lane in range(1, 16):
            total = total + piece_ref[g, 1 - parity, lane].astype(F32)
        sums.append(total)
    mine = jnp.concatenate(sums, axis=0).astype(BF)
    for r in range(128):
        out_ref[r] = mine
    info_ref[...] = piece_ref[grp // 2, parity]


def apply_level(level, blocks, place, xbd_ref, yw_ref, zw_ref, spread_ref, table_ref, acc_ref):
    xbd = xbd_ref[level]

    def prepare(cyz):
        cy, cz, slot = cyz // 3, cyz % 3, cyz % 2
        for group in range(SLOT // GROUP):
            parts = []
            for b in range(group * GROUP, (group + 1) * GROUP):
                for cx in range(3):
                    at = pl.multiple_of(place(b, 9 * cx + cyz), 32)
                    parts.append(
                        jnp.concatenate(
                            [blocks[pl.ds(at, 16), :], blocks[pl.ds(at + 16, 16), :]], axis=1
                        )
                    )
            spread = dot(xbd, jnp.concatenate(parts, axis=0)).astype(BF)
            for m in range(TERMS):
                size = GROUP * K
                spread_ref[slot, group * size : (group + 1) * size, m * KK : (m + 1) * KK] = (
                    spread[m * size : (m + 1) * size, :]
                )
        for m in range(TERMS):
            zpart = zw_ref[level, m * 3 + cz]
            ypart = yw_ref[level, m * 3 + cy]
            for r in range(K):
                table_ref[slot, m * KK + r * K : m * KK + (r + 1) * K, :] = (
                    ypart[r : r + 1, :] * zpart
                ).astype(BF)

    prepare(0)
    for cyz in range(9):
        if cyz < 8:
            prepare(cyz + 1)
        term = dot(spread_ref[cyz % 2], table_ref[cyz % 2])
        acc_ref[...] = term if cyz == 0 else acc_ref[...] + term


def fine_kernel(
    idx_ref,
    counts_ref,
    arrived_ref,
    fine_ref,
    info_ref,
    xbd_ref,
    yw_ref,
    zw_ref,
    out_ref,
    one_ref,
    coarse_idx_ref,
    pool_ref,
    spread_ref,
    table_ref,
    acc_ref,
    sems,
):
    copies = []
    for level in range(2):
        part = pl.ds(level * 64, 64)
        copies.append(
            pltpu.make_async_copy(
                arrived_ref.at[:, part], pool_ref.at[pl.ds(0, 128), part], sems.at[level]
            )
        )
        copies[-1].start()
    for level in range(2):
        for b in range(SLOT):
            block = fine_ref[level, b]
            pool_ref[128 + b, level * 64 : level * 64 + 16, :] = block[:, 0:128]
            pool_ref[128 + b, level * 64 + 16 : level * 64 + 32, :] = block[:, 128:256]
    pool_ref[144, 0:32, :] = jnp.zeros((32, 128), BF)
    lists = info_ref[...].astype(F32)
    refs, codes, mask = (lists[:, i, :] for i in range(3))
    codes = jnp.where(mask == 1.0, codes, -1.0)
    offset = iota((16, 128), 1).astype(F32)
    place = jnp.full((16, 128), 128.0, F32)
    for j in range(16):
        place = jnp.where(codes[:, j : j + 1] == offset, refs[:, j : j + 1], place)
    coarse_idx_ref[...] = place.astype(jnp.int32) * 32

    blocks = pool_ref.reshape(145 * 128, 128)

    for level in range(2):
        copies[level].wait()
        apply_level(
            level,
            blocks,
            lambda b, code: idx_ref[(level * SLOT + b) * CODES + code],
            xbd_ref,
            yw_ref,
            zw_ref,
            spread_ref,
            table_ref,
            acc_ref,
        )
        for b in range(SLOT):
            rows = jnp.where(b < counts_ref[level, 0], acc_ref[b * K : (b + 1) * K, :], 0.0)
            if level == 0:
                out_ref[0, b] = rows.astype(BF)
            else:
                one_ref[b] = rows


def tail_kernel(
    idx_ref,
    parent_ref,
    code_ref,
    summed_ref,
    one_ref,
    xbd_ref,
    yw_ref,
    zw_ref,
    filt_ref,
    fine_in_ref,
    fine_out_ref,
    coarse_out_ref,
    pool_ref,
    spread_ref,
    table_ref,
    acc_ref,
    coarse_ref,
    result_ref,
    sems,
):
    copies = []
    for g in range(8):
        copies.append(
            pltpu.make_async_copy(
                summed_ref.at[:, 1 - g % 2, g // 2], pool_ref.at[g], sems.at[g]
            )
        )
        copies[-1].start()
    pool_ref[8, 0:4] = jnp.zeros((4, 8, 128), BF)
    blocks = pool_ref.reshape(9 * 512, 128)
    for copy in copies:
        copy.wait()

    apply_level(
        2,
        blocks,
        lambda b, code: idx_ref[b, code],
        xbd_ref,
        yw_ref,
        zw_ref,
        spread_ref,
        table_ref,
        acc_ref,
    )
    for t in range(SLOT):
        coarse_ref[t] = acc_ref[t * K : (t + 1) * K, :]
    coarse_out_ref[0] = coarse_ref[lax.axis_index("lane")].astype(BF)

    rep_n, tile_n, _, tile_t = factors(filt_ref)
    lane_block = iota((K, KK), 1) // K
    rows = []
    for b in range(SLOT):
        chosen = jnp.where(code_ref[b] // 4 == 1, tile_t[1], tile_t[0])
        rows.append(jnp.where(lane_block == parent_ref[b], chosen, 0.0).astype(BF))
    lowered = dot(jnp.concatenate(rows, axis=0), acc_ref[...].astype(BF)).astype(BF)
    correction = dot(corner_spread(lowered, code_ref), corner_tables(rep_n, tile_n))
    for b in range(SLOT):
        result_ref[b] = (one_ref[b] + correction[b * K : (b + 1) * K, :]).astype(BF)
    copy = pltpu.make_async_copy(result_ref, fine_out_ref.at[1], sems.at[8])
    copy.start()
    copy.wait()


def smem():
    return pl.BlockSpec(memory_space=pltpu.SMEM)


def vmem():
    return pl.BlockSpec(memory_space=pltpu.VMEM)


def room(mib):
    return pltpu.CompilerParams(vmem_limit_bytes=mib * 1024 * 1024)


def anywhere():
    return pl.BlockSpec(memory_space=pl.ANY)


def code_index(codes, mask, places, empty):
    hits = (codes[:, None, :] == jnp.arange(CODES, dtype=jnp.int32)[None, :, None]) & (
        mask[:, None, :] == 1
    )
    return empty + jnp.sum(jnp.where(hits, places[:, None, :] - empty, 0), axis=2)


def body(
    fine_in,
    counts,
    neighbour_refs,
    offset_codes,
    neighbour_mask,
    send_slots,
    parent_of,
    child_code,
    coarse_refs,
    coarse_codes,
    coarse_mask,
    ops_x,
    ops_y,
    ops_z,
    filters,
):
    send = pl.pallas_call(
        send_kernel,
        in_specs=[smem()] * 3 + [vmem()] * 5,
        out_specs=anywhere(),
        out_shape=jax.ShapeDtypeStruct((128, 136, 128), BF),
        scratch_shapes=[
            pltpu.VMEM((128, 128, 128), BF),
            pltpu.VMEM((128, 8, 128), BF),
            pltpu.VMEM((SLOT + 1, K, KK), F32),
            pltpu.SemaphoreType.DMA((9,)),
        ],
        name="send",
    )(
        parent_of,
        child_code,
        send_slots,
        fine_in,
        filters,
        coarse_refs,
        coarse_codes,
        coarse_mask,
    )
    arrived = lax.all_to_all(send, AXES, split_axis=0, concat_axis=0, tiled=True)

    summed, info = pl.pallas_call(
        place_kernel,
        in_specs=[anywhere()],
        out_specs=[vmem(), vmem()],
        out_shape=[
            jax.ShapeDtypeStruct((128, 32, 128), BF),
            jax.ShapeDtypeStruct((16, 8, 128), BF),
        ],
        scratch_shapes=[pltpu.VMEM((4, 2, 16, 8, 128), BF), pltpu.SemaphoreType.DMA],
        compiler_params=room(8),
        name="place",
    )(arrived.reshape(4, 2, 16, 136, 128))
    summed = lax.all_to_all(summed, AXES[::-1], split_axis=0, concat_axis=0, tiled=True)

    repeat, tiled = spreads()
    yw = jnp.einsum("lmcpr,pk->lmcrk", ops_y, repeat, preferred_element_type=F32)
    zw = jnp.einsum("lmcqs,qk->lmcsk", ops_z, tiled, preferred_element_type=F32)
    yw = yw.reshape(3, 12, K, KK)
    zw = zw.reshape(3, 12, K, KK)
    xm = jnp.transpose(ops_x, (0, 1, 3, 2, 4)).reshape(3, 64, 48)
    size = GROUP * K
    row, col = iota((4 * size, 64), 0), iota((4 * size, 64), 1)
    grow = ((row // size == col // K) & (row % K == col % K)).astype(BF)
    row, col = iota((48, 3 * size), 0), iota((48, 3 * size), 1)
    wide = (col % 48 == row).astype(BF)
    row, col = iota((4 * size, 3 * size), 0), iota((4 * size, 3 * size), 1)
    own = (row % size) // K == col // 48
    xbd = jnp.einsum("ij,ljk->lik", grow, xm)
    xbd = jnp.einsum("lik,kn->lin", xbd, wide)
    xbd = jnp.where(own[None], xbd, jnp.zeros_like(xbd))

    empty = 144 * 128
    tables = []
    for level in range(2):
        refs = neighbour_refs[level]
        far = refs - SLOT
        places = jnp.where(
            refs < SLOT,
            (128 + refs) * 128 + level * 64,
            (far // CAP) * 128 + level * 64 + (far % CAP) * 32,
        )
        tables.append(code_index(offset_codes[level], neighbour_mask[level], places, empty))
    idx = jnp.concatenate([t.reshape(-1) for t in tables])
    work = [
        pltpu.VMEM((2, KK, TERMS * KK), BF),
        pltpu.VMEM((2, TERMS * KK, KK), BF),
        pltpu.VMEM((KK, KK), F32),
    ]
    fine_out, one, coarse_idx = pl.pallas_call(
        fine_kernel,
        in_specs=[smem()] * 2 + [anywhere()] + [vmem()] * 5,
        out_specs=[pl.BlockSpec((1, SLOT, K, KK), lambda i: (0, 0, 0, 0)), vmem(), vmem()],
        out_shape=[
            jax.ShapeDtypeStruct((2, SLOT, K, KK), BF),
            jax.ShapeDtypeStruct((SLOT, K, KK), F32),
            jax.ShapeDtypeStruct((16, 128), jnp.int32),
        ],
        grid=(1,),
        scratch_shapes=[pltpu.VMEM((145, 128, 128), BF)]
        + work
        + [pltpu.SemaphoreType.DMA((2,))],
        compiler_params=room(20),
        name="fine",
        cost_estimate=pl.CostEstimate(
            flops=10_000_000_000, bytes_accessed=6_000_000, transcendentals=0
        ),
    )(idx, counts, arrived, fine_in, info, xbd, yw, zw)

    fine_out, coarse_out = pl.pallas_call(
        tail_kernel,
        in_specs=[smem()] * 3 + [anywhere()] + [vmem()] * 5 + [anywhere()],
        out_specs=[anywhere(), vmem()],
        out_shape=[
            jax.ShapeDtypeStruct((2, SLOT, K, KK), BF),
            jax.ShapeDtypeStruct((1, K, KK), BF),
        ],
        scratch_shapes=[pltpu.VMEM((9, 64, 8, 128), BF)]
        + work
        + [
            pltpu.VMEM((SLOT, K, KK), F32),
            pltpu.VMEM((SLOT, K, KK), BF),
            pltpu.SemaphoreType.DMA((9,)),
        ],
        input_output_aliases={9: 0},
        compiler_params=room(16),
        name="tail",
    )(
        coarse_idx,
        parent_of,
        child_code,
        summed.reshape(64, 2, 4, 8, 128),
        one,
        xbd,
        yw,
        zw,
        filters,
        fine_out,
    )
    return fine_out, coarse_out


def solution(mesh):
    blocks = P(None, AXES, None, None)
    table = P(None, AXES, None)
    in_specs = (
        blocks,
        P(None, AXES),
        table,
        table,
        table,
        table,
        P(AXES),
        P(AXES),
        P(AXES, None),
        P(AXES, None),
        P(AXES, None),
        P(),
        P(),
        P(),
        P(),
    )
    out_specs = (blocks, P(AXES, None, None))
    return jax.shard_map(body, mesh=mesh, in_specs=in_specs, out_specs=out_specs, check_vma=False)
```

```python
import jax
import jax.numpy as jnp
from jax import lax
from jax.experimental import pallas as pl
from jax.experimental.pallas import tpu as pltpu
from jax.sharding import PartitionSpec as P

K = 16
KK = K * K
TERMS = 4
SLOT = 16
CAP = 2
CODES = 27
GROUP = 4
BF = jnp.bfloat16
F32 = jnp.float32
AXES = ("y", "core", "lane")


def iota(shape, dim):
    return lax.broadcasted_iota(jnp.int32, shape, dim)


def spreads():
    row, col = iota((K, KK), 0), iota((K, KK), 1)
    return (col // K == row).astype(BF), (col % K == row).astype(BF)


def dot(a, b):
    return jnp.dot(a, b, preferred_element_type=F32)


def corner_tables(rep, tile):
    rows = []
    for cy in range(2):
        for cz in range(2):
            for p in range(K):
                rows.append((rep[cy][p : p + 1, :] * tile[cz]).astype(BF))
    return jnp.concatenate(rows, axis=0)


def corner_spread(blocks, code_ref):
    columns = []
    for corner in range(4):
        rows = []
        for b in range(SLOT):
            part = blocks[b * K : (b + 1) * K, :]
            rows.append(jnp.where(code_ref[b] % 4 == corner, part, jnp.zeros_like(part)))
        columns.append(jnp.concatenate(rows, axis=0))
    return jnp.concatenate(columns, axis=1)


def factors(filt_ref):
    repeat, tiled = spreads()
    flip = lambda f, e: lax.dot_general(f, e, (((0,), (0,)), ((), ())), preferred_element_type=F32)
    filts = [filt_ref[c] for c in range(2)]
    rep_n = [dot(f, repeat) for f in filts]
    tile_n = [dot(f, tiled) for f in filts]
    rep_t = [flip(f, repeat) for f in filts]
    tile_t = [flip(f, tiled) for f in filts]
    return rep_n, tile_n, rep_t, tile_t


def send_kernel(
    parent_ref,
    code_ref,
    slots_ref,
    fine_ref,
    filt_ref,
    refs_ref,
    codes_ref,
    mask_ref,
    send_ref,
    pack_ref,
    piece_ref,
    acc_ref,
    sems,
):
    copies = []
    for chunk in range(8):

        def fill(r, carry):
            for level in range(2):
                for c in range(CAP):
                    slot = slots_ref[level, 0, r * CAP + c]
                    at = 32 * (level * CAP + c)
                    block = fine_ref[level, slot]
                    pack_ref[r, at : at + 16, :] = block[:, 0:128]
                    pack_ref[r, at + 16 : at + 32, :] = block[:, 128:256]
            return carry

        lax.fori_loop(chunk * 16, chunk * 16 + 16, fill, 0, unroll=4)
        here = pl.ds(chunk * 16, 16)
        copies.append(
            pltpu.make_async_copy(
                pack_ref.at[here], send_ref.at[here, pl.ds(0, 128)], sems.at[chunk]
            )
        )
        copies[-1].start()

    _, tile_n, rep_t, tile_t = factors(filt_ref)
    lane_block = iota((K, KK), 1) // K
    rows = []
    for b in range(SLOT):
        chosen = jnp.where(code_ref[b] // 4 == 1, tile_n[1], tile_n[0])
        rows.append(jnp.where(lane_block == b, chosen, 0.0).astype(BF))
    lifted = dot(jnp.concatenate(rows, axis=0), fine_ref[1].reshape(SLOT * K, KK)).astype(BF)
    moved = dot(corner_spread(lifted, code_ref), corner_tables(rep_t, tile_t))
    parity = lax.axis_index("core")
    info = jnp.concatenate([refs_ref[...], codes_ref[...]] + [mask_ref[...]] * 6, axis=0)
    wide = (iota((16, 128), 0) == iota((16, 128), 1)).astype(BF)
    info = dot(info.astype(F32).astype(BF), wide).astype(BF)
    for gp in range(4):
        for lane in range(16):
            piece_ref[(2 * gp + parity) * 16 + lane] = info
    acc_ref[...] = jnp.zeros_like(acc_ref)
    for b in range(SLOT):
        parent = parent_ref[b]
        target = jnp.where(parent < 0, SLOT, parent)
        acc_ref[target] = acc_ref[target] + moved[b * K : (b + 1) * K, :]
    for t in range(SLOT):
        for half in range(2):
            for top in range(2):
                tile = acc_ref[t, top * 8 : top * 8 + 8, half * 128 : half * 128 + 128].astype(BF)
                j = t * 4 + half * 2 + top
                piece_ref[(2 * (j % 4) + 1 - parity) * 16 + j // 4] = tile
    copies.append(
        pltpu.make_async_copy(piece_ref, send_ref.at[:, pl.ds(128, 8)], sems.at[8])
    )
    copies[-1].start()
    for copy in copies:
        copy.wait()


def place_kernel(arrived_ref, out_ref, info_ref, piece_ref, sem):
    parity = lax.axis_index("core")
    copy = pltpu.make_async_copy(arrived_ref.at[:, :, :, pl.ds(128, 8)], piece_ref, sem)
    copy.start()
    copy.wait()
    sums = []
    for g in range(4):
        total = piece_ref[g, 1 - parity, 0].astype(F32)
        for lane in range(1, 16):
            total = total + piece_ref[g, 1 - parity, lane].astype(F32)
        sums.append(total)
    mine = jnp.concatenate(sums, axis=0).astype(BF)
    for r in range(64):
        out_ref[r] = mine
    info_ref[...] = piece_ref[lax.axis_index("y"), parity]


def apply_level(level, blocks, place, xbd_ref, yw_ref, zw_ref, spread_ref, table_ref, acc_ref):
    xbd = xbd_ref[level]

    def prepare(cyz):
        cy, cz, slot = cyz // 3, cyz % 3, cyz % 2
        for group in range(SLOT // GROUP):
            parts = []
            for b in range(group * GROUP, (group + 1) * GROUP):
                for cx in range(3):
                    at = pl.multiple_of(place(b, 9 * cx + cyz), 32)
                    parts.append(
                        jnp.concatenate(
                            [blocks[pl.ds(at, 16), :], blocks[pl.ds(at + 16, 16), :]], axis=1
                        )
                    )
            spread = dot(xbd, jnp.concatenate(parts, axis=0)).astype(BF)
            for m in range(TERMS):
                size = GROUP * K
                spread_ref[slot, group * size : (group + 1) * size, m * KK : (m + 1) * KK] = (
                    spread[m * size : (m + 1) * size, :]
                )
        for m in range(TERMS):
            zpart = zw_ref[level, m * 3 + cz]
            ypart = yw_ref[level, m * 3 + cy]
            for r in range(K):
                table_ref[slot, m * KK + r * K : m * KK + (r + 1) * K, :] = (
                    ypart[r : r + 1, :] * zpart
                ).astype(BF)

    prepare(0)
    for cyz in range(9):
        if cyz < 8:
            prepare(cyz + 1)
        term = dot(spread_ref[cyz % 2], table_ref[cyz % 2])
        acc_ref[...] = term if cyz == 0 else acc_ref[...] + term


def fine_kernel(
    idx_ref,
    counts_ref,
    arrived_ref,
    fine_ref,
    info_ref,
    xbd_ref,
    yw_ref,
    zw_ref,
    out_ref,
    one_ref,
    coarse_idx_ref,
    pool_ref,
    spread_ref,
    table_ref,
    acc_ref,
    sems,
):
    copies = []
    for level in range(2):
        part = pl.ds(level * 64, 64)
        copies.append(
            pltpu.make_async_copy(
                arrived_ref.at[:, part], pool_ref.at[pl.ds(0, 128), part], sems.at[level]
            )
        )
        copies[-1].start()
    for level in range(2):
        for b in range(SLOT):
            block = fine_ref[level, b]
            pool_ref[128 + b, level * 64 : level * 64 + 16, :] = block[:, 0:128]
            pool_ref[128 + b, level * 64 + 16 : level * 64 + 32, :] = block[:, 128:256]
    pool_ref[144, 0:32, :] = jnp.zeros((32, 128), BF)
    lists = info_ref[...].astype(F32)
    refs, codes, mask = (lists[:, i, :] for i in range(3))
    codes = jnp.where(mask == 1.0, codes, -1.0)
    offset = iota((16, 128), 1).astype(F32)
    place = jnp.full((16, 128), 128.0, F32)
    for j in range(16):
        place = jnp.where(codes[:, j : j + 1] == offset, refs[:, j : j + 1], place)
    coarse_idx_ref[...] = place.astype(jnp.int32) * 32

    blocks = pool_ref.reshape(145 * 128, 128)

    for level in range(2):
        copies[level].wait()
        apply_level(
            level,
            blocks,
            lambda b, code: idx_ref[(level * SLOT + b) * CODES + code],
            xbd_ref,
            yw_ref,
            zw_ref,
            spread_ref,
            table_ref,
            acc_ref,
        )
        for b in range(SLOT):
            rows = jnp.where(b < counts_ref[level, 0], acc_ref[b * K : (b + 1) * K, :], 0.0)
            if level == 0:
                out_ref[0, b] = rows.astype(BF)
            else:
                one_ref[b] = rows


def tail_kernel(
    idx_ref,
    parent_ref,
    code_ref,
    summed_ref,
    other_ref,
    one_ref,
    xbd_ref,
    yw_ref,
    zw_ref,
    filt_ref,
    fine_in_ref,
    fine_out_ref,
    coarse_out_ref,
    pool_ref,
    spread_ref,
    table_ref,
    acc_ref,
    coarse_ref,
    result_ref,
    sems,
):
    copies = []
    parity = lax.axis_index("core")
    for gp in range(4):
        for ref, side in ((summed_ref, 1 - parity), (other_ref, parity)):
            copies.append(
                pltpu.make_async_copy(
                    ref.at[:, gp], pool_ref.at[2 * gp + side], sems.at[len(copies)]
                )
            )
            copies[-1].start()
    pool_ref[8, 0:4] = jnp.zeros((4, 8, 128), BF)
    blocks = pool_ref.reshape(9 * 512, 128)
    for copy in copies:
        copy.wait()

    apply_level(
        2,
        blocks,
        lambda b, code: idx_ref[b, code],
        xbd_ref,
        yw_ref,
        zw_ref,
        spread_ref,
        table_ref,
        acc_ref,
    )
    for t in range(SLOT):
        coarse_ref[t] = acc_ref[t * K : (t + 1) * K, :]
    coarse_out_ref[0] = coarse_ref[lax.axis_index("lane")].astype(BF)

    rep_n, tile_n, _, tile_t = factors(filt_ref)
    lane_block = iota((K, KK), 1) // K
    rows = []
    for b in range(SLOT):
        chosen = jnp.where(code_ref[b] // 4 == 1, tile_t[1], tile_t[0])
        rows.append(jnp.where(lane_block == parent_ref[b], chosen, 0.0).astype(BF))
    lowered = dot(jnp.concatenate(rows, axis=0), acc_ref[...].astype(BF)).astype(BF)
    correction = dot(corner_spread(lowered, code_ref), corner_tables(rep_n, tile_n))
    for b in range(SLOT):
        result_ref[b] = (one_ref[b] + correction[b * K : (b + 1) * K, :]).astype(BF)
    copy = pltpu.make_async_copy(result_ref, fine_out_ref.at[1], sems.at[8])
    copy.start()
    copy.wait()


def smem():
    return pl.BlockSpec(memory_space=pltpu.SMEM)


def vmem():
    return pl.BlockSpec(memory_space=pltpu.VMEM)


def room(mib):
    return pltpu.CompilerParams(vmem_limit_bytes=mib * 1024 * 1024)


def anywhere():
    return pl.BlockSpec(memory_space=pl.ANY)


def code_index(codes, mask, places, empty):
    hits = (codes[:, None, :] == jnp.arange(CODES, dtype=jnp.int32)[None, :, None]) & (
        mask[:, None, :] == 1
    )
    return empty + jnp.sum(jnp.where(hits, places[:, None, :] - empty, 0), axis=2)


def body(
    fine_in,
    counts,
    neighbour_refs,
    offset_codes,
    neighbour_mask,
    send_slots,
    parent_of,
    child_code,
    coarse_refs,
    coarse_codes,
    coarse_mask,
    ops_x,
    ops_y,
    ops_z,
    filters,
):
    send = pl.pallas_call(
        send_kernel,
        in_specs=[smem()] * 3 + [vmem()] * 5,
        out_specs=anywhere(),
        out_shape=jax.ShapeDtypeStruct((128, 136, 128), BF),
        scratch_shapes=[
            pltpu.VMEM((128, 128, 128), BF),
            pltpu.VMEM((128, 8, 128), BF),
            pltpu.VMEM((SLOT + 1, K, KK), F32),
            pltpu.SemaphoreType.DMA((9,)),
        ],
        name="send",
    )(
        parent_of,
        child_code,
        send_slots,
        fine_in,
        filters,
        coarse_refs,
        coarse_codes,
        coarse_mask,
    )
    arrived = lax.all_to_all(send, AXES, split_axis=0, concat_axis=0, tiled=True)

    summed, info = pl.pallas_call(
        place_kernel,
        in_specs=[anywhere()],
        out_specs=[vmem(), vmem()],
        out_shape=[
            jax.ShapeDtypeStruct((64, 32, 128), BF),
            jax.ShapeDtypeStruct((16, 8, 128), BF),
        ],
        scratch_shapes=[pltpu.VMEM((4, 2, 16, 8, 128), BF), pltpu.SemaphoreType.DMA],
        compiler_params=room(8),
        name="place",
    )(arrived.reshape(4, 2, 16, 136, 128))
    summed = lax.all_to_all(summed, ("lane", "y"), split_axis=0, concat_axis=0, tiled=True)

    repeat, tiled = spreads()
    yw = jnp.einsum("lmcpr,pk->lmcrk", ops_y, repeat, preferred_element_type=F32)
    zw = jnp.einsum("lmcqs,qk->lmcsk", ops_z, tiled, preferred_element_type=F32)
    yw = yw.reshape(3, 12, K, KK)
    zw = zw.reshape(3, 12, K, KK)
    xm = jnp.transpose(ops_x, (0, 1, 3, 2, 4)).reshape(3, 64, 48)
    size = GROUP * K
    row, col = iota((4 * size, 64), 0), iota((4 * size, 64), 1)
    grow = ((row // size == col // K) & (row % K == col % K)).astype(BF)
    row, col = iota((48, 3 * size), 0), iota((48, 3 * size), 1)
    wide = (col % 48 == row).astype(BF)
    row, col = iota((4 * size, 3 * size), 0), iota((4 * size, 3 * size), 1)
    own = (row % size) // K == col // 48
    xbd = jnp.einsum("ij,ljk->lik", grow, xm)
    xbd = jnp.einsum("lik,kn->lin", xbd, wide)
    xbd = jnp.where(own[None], xbd, jnp.zeros_like(xbd))

    empty = 144 * 128
    tables = []
    for level in range(2):
        refs = neighbour_refs[level]
        far = refs - SLOT
        places = jnp.where(
            refs < SLOT,
            (128 + refs) * 128 + level * 64,
            (far // CAP) * 128 + level * 64 + (far % CAP) * 32,
        )
        tables.append(code_index(offset_codes[level], neighbour_mask[level], places, empty))
    idx = jnp.concatenate([t.reshape(-1) for t in tables])
    work = [
        pltpu.VMEM((2, KK, TERMS * KK), BF),
        pltpu.VMEM((2, TERMS * KK, KK), BF),
        pltpu.VMEM((KK, KK), F32),
    ]
    fine_out, one, coarse_idx = pl.pallas_call(
        fine_kernel,
        in_specs=[smem()] * 2 + [anywhere()] + [vmem()] * 5,
        out_specs=[pl.BlockSpec((1, SLOT, K, KK), lambda i: (0, 0, 0, 0)), vmem(), vmem()],
        out_shape=[
            jax.ShapeDtypeStruct((2, SLOT, K, KK), BF),
            jax.ShapeDtypeStruct((SLOT, K, KK), F32),
            jax.ShapeDtypeStruct((16, 128), jnp.int32),
        ],
        grid=(1,),
        scratch_shapes=[pltpu.VMEM((145, 128, 128), BF)]
        + work
        + [pltpu.SemaphoreType.DMA((2,))],
        compiler_params=room(20),
        name="fine",
        cost_estimate=pl.CostEstimate(
            flops=10_000_000_000, bytes_accessed=6_000_000, transcendentals=0
        ),
    )(idx, counts, arrived, fine_in, info, xbd, yw, zw)

    summed, coarse_idx = lax.optimization_barrier((summed, coarse_idx))
    other = lax.ppermute(summed, "core", [(0, 1), (1, 0)])
    fine_out, coarse_out = pl.pallas_call(
        tail_kernel,
        in_specs=[smem()] * 3 + [anywhere()] * 2 + [vmem()] * 5 + [anywhere()],
        out_specs=[anywhere(), vmem()],
        out_shape=[
            jax.ShapeDtypeStruct((2, SLOT, K, KK), BF),
            jax.ShapeDtypeStruct((1, K, KK), BF),
        ],
        scratch_shapes=[pltpu.VMEM((9, 64, 8, 128), BF)]
        + work
        + [
            pltpu.VMEM((SLOT, K, KK), F32),
            pltpu.VMEM((SLOT, K, KK), BF),
            pltpu.SemaphoreType.DMA((9,)),
        ],
        input_output_aliases={10: 0},
        compiler_params=room(16),
        name="tail",
    )(
        coarse_idx,
        parent_of,
        child_code,
        summed.reshape(64, 4, 8, 128),
        other.reshape(64, 4, 8, 128),
        one,
        xbd,
        yw,
        zw,
        filters,
        fine_out,
    )
    return fine_out, coarse_out


def solution(mesh):
    blocks = P(None, AXES, None, None)
    table = P(None, AXES, None)
    in_specs = (
        blocks,
        P(None, AXES),
        table,
        table,
        table,
        table,
        P(AXES),
        P(AXES),
        P(AXES, None),
        P(AXES, None),
        P(AXES, None),
        P(),
        P(),
        P(),
        P(),
    )
    out_specs = (blocks, P(AXES, None, None))
    parts = (mesh.shape["grp"] // 2, 2, mesh.shape["lane"])
    mesh = jax.sharding.Mesh(mesh.devices.reshape(parts), AXES)
    return jax.shard_map(body, mesh=mesh, in_specs=in_specs, out_specs=out_specs, check_vma=False)
```

```python
import jax
import jax.numpy as jnp
from jax import lax
from jax.experimental import pallas as pl
from jax.experimental.pallas import tpu as pltpu
from jax.sharding import PartitionSpec as P

K = 16
KK = K * K
TERMS = 4
SLOT = 16
CAP = 2
CODES = 27
GROUP = 4
BF = jnp.bfloat16
F32 = jnp.float32
AXES = ("y", "core", "lane")


def iota(shape, dim):
    return lax.broadcasted_iota(jnp.int32, shape, dim)


def spreads():
    row, col = iota((K, KK), 0), iota((K, KK), 1)
    return (col // K == row).astype(BF), (col % K == row).astype(BF)


def dot(a, b):
    return jnp.dot(a, b, preferred_element_type=F32)


def corner_tables(rep, tile):
    rows = []
    for cy in range(2):
        for cz in range(2):
            for p in range(K):
                rows.append((rep[cy][p : p + 1, :] * tile[cz]).astype(BF))
    return jnp.concatenate(rows, axis=0)


def corner_spread(blocks, code_ref):
    columns = []
    for corner in range(4):
        rows = []
        for b in range(SLOT):
            part = blocks[b * K : (b + 1) * K, :]
            rows.append(jnp.where(code_ref[b] % 4 == corner, part, jnp.zeros_like(part)))
        columns.append(jnp.concatenate(rows, axis=0))
    return jnp.concatenate(columns, axis=1)


def factors(filt_ref):
    repeat, tiled = spreads()
    flip = lambda f, e: lax.dot_general(f, e, (((0,), (0,)), ((), ())), preferred_element_type=F32)
    filts = [filt_ref[c] for c in range(2)]
    rep_n = [dot(f, repeat) for f in filts]
    tile_n = [dot(f, tiled) for f in filts]
    rep_t = [flip(f, repeat) for f in filts]
    tile_t = [flip(f, tiled) for f in filts]
    return rep_n, tile_n, rep_t, tile_t


def send_kernel(
    parent_ref,
    code_ref,
    slots_ref,
    fine_ref,
    filt_ref,
    refs_ref,
    codes_ref,
    mask_ref,
    send_ref,
    pack_ref,
    piece_ref,
    acc_ref,
    sems,
):
    copies = []
    for chunk in range(8):

        def fill(r, carry):
            for level in range(2):
                for c in range(CAP):
                    slot = slots_ref[level, 0, r * CAP + c]
                    at = 32 * (level * CAP + c)
                    block = fine_ref[level, slot]
                    pack_ref[r, at : at + 16, :] = block[:, 0:128]
                    pack_ref[r, at + 16 : at + 32, :] = block[:, 128:256]
            return carry

        lax.fori_loop(chunk * 16, chunk * 16 + 16, fill, 0, unroll=4)
        here = pl.ds(chunk * 16, 16)
        copies.append(
            pltpu.make_async_copy(
                pack_ref.at[here], send_ref.at[here, pl.ds(0, 128)], sems.at[chunk]
            )
        )
        copies[-1].start()

    _, tile_n, rep_t, tile_t = factors(filt_ref)
    lane_block = iota((K, KK), 1) // K
    rows = []
    for b in range(SLOT):
        chosen = jnp.where(code_ref[b] // 4 == 1, tile_n[1], tile_n[0])
        rows.append(jnp.where(lane_block == b, chosen, 0.0).astype(BF))
    lifted = dot(jnp.concatenate(rows, axis=0), fine_ref[1].reshape(SLOT * K, KK)).astype(BF)
    moved = dot(corner_spread(lifted, code_ref), corner_tables(rep_t, tile_t))
    parity = lax.axis_index("core")
    info = jnp.concatenate([refs_ref[...], codes_ref[...]] + [mask_ref[...]] * 6, axis=0)
    wide = (iota((16, 128), 0) == iota((16, 128), 1)).astype(BF)
    info = dot(info.astype(F32).astype(BF), wide).astype(BF)
    for gp in range(4):
        for lane in range(16):
            piece_ref[(2 * gp + parity) * 16 + lane] = info
    acc_ref[...] = jnp.zeros_like(acc_ref)
    for b in range(SLOT):
        parent = parent_ref[b]
        target = jnp.where(parent < 0, SLOT, parent)
        acc_ref[target] = acc_ref[target] + moved[b * K : (b + 1) * K, :]
    for t in range(SLOT):
        for half in range(2):
            for top in range(2):
                tile = acc_ref[t, top * 8 : top * 8 + 8, half * 128 : half * 128 + 128].astype(BF)
                j = t * 4 + half * 2 + top
                piece_ref[(2 * (j % 4) + 1 - parity) * 16 + j // 4] = tile
    copies.append(
        pltpu.make_async_copy(piece_ref, send_ref.at[:, pl.ds(128, 8)], sems.at[8])
    )
    copies[-1].start()
    for copy in copies:
        copy.wait()


def place_kernel(arrived_ref, out_ref, info_ref, piece_ref, copies_ref, sems):
    parity = lax.axis_index("core")
    tile = pl.ds(128, 8)
    pieces = pltpu.make_async_copy(arrived_ref.at[:, 1 - parity, :, tile], piece_ref, sems.at[0])
    pieces.start()
    lists = pltpu.make_async_copy(
        arrived_ref.at[lax.axis_index("y"), parity, :, tile], info_ref, sems.at[1]
    )
    lists.start()
    pieces.wait()
    sums = []
    for g in range(4):
        total = piece_ref[g, 0].astype(F32)
        for lane in range(1, 16):
            total = total + piece_ref[g, lane].astype(F32)
        sums.append(total)
    mine = jnp.concatenate(sums, axis=0).astype(BF)
    for r in range(16):
        copies_ref[r] = mine
    sends = [
        pltpu.make_async_copy(copies_ref, out_ref.at[pl.ds(16 * i, 16)], sems.at[2 + i])
        for i in range(4)
    ]
    for send in sends:
        send.start()
    lists.wait()
    for send in sends:
        send.wait()


def apply_level(level, blocks, place, xbd_ref, yw_ref, zw_ref, spread_ref, table_ref, acc_ref):
    xbd = xbd_ref[level]

    def prepare(cyz):
        cy, cz, slot = cyz // 3, cyz % 3, cyz % 2
        for group in range(SLOT // GROUP):
            parts = []
            for b in range(group * GROUP, (group + 1) * GROUP):
                for cx in range(3):
                    at = pl.multiple_of(place(b, 9 * cx + cyz), 32)
                    parts.append(
                        jnp.concatenate(
                            [blocks[pl.ds(at, 16), :], blocks[pl.ds(at + 16, 16), :]], axis=1
                        )
                    )
            spread = dot(xbd, jnp.concatenate(parts, axis=0)).astype(BF)
            for m in range(TERMS):
                size = GROUP * K
                spread_ref[slot, group * size : (group + 1) * size, m * KK : (m + 1) * KK] = (
                    spread[m * size : (m + 1) * size, :]
                )
        for m in range(TERMS):
            zpart = zw_ref[level, m * 3 + cz]
            ypart = yw_ref[level, m * 3 + cy]
            for r in range(K):
                table_ref[slot, m * KK + r * K : m * KK + (r + 1) * K, :] = (
                    ypart[r : r + 1, :] * zpart
                ).astype(BF)

    prepare(0)
    for cyz in range(9):
        if cyz < 8:
            prepare(cyz + 1)
        term = dot(spread_ref[cyz % 2], table_ref[cyz % 2])
        acc_ref[...] = term if cyz == 0 else acc_ref[...] + term


def fine_kernel(
    idx_ref,
    counts_ref,
    arrived_ref,
    fine_ref,
    info_ref,
    xbd_ref,
    yw_ref,
    zw_ref,
    out_ref,
    one_ref,
    coarse_idx_ref,
    pool_ref,
    spread_ref,
    table_ref,
    acc_ref,
    sems,
):
    copies = []
    for level in range(2):
        part = pl.ds(level * 64, 64)
        copies.append(
            pltpu.make_async_copy(
                arrived_ref.at[:, part], pool_ref.at[pl.ds(0, 128), part], sems.at[level]
            )
        )
        copies[-1].start()
    for level in range(2):
        for b in range(SLOT):
            block = fine_ref[level, b]
            pool_ref[128 + b, level * 64 : level * 64 + 16, :] = block[:, 0:128]
            pool_ref[128 + b, level * 64 + 16 : level * 64 + 32, :] = block[:, 128:256]
    pool_ref[144, 0:32, :] = jnp.zeros((32, 128), BF)
    lists = info_ref[...].astype(F32)
    refs, codes, mask = (lists[:, i, :] for i in range(3))
    codes = jnp.where(mask == 1.0, codes, -1.0)
    offset = iota((16, 128), 1).astype(F32)
    place = jnp.full((16, 128), 128.0, F32)
    for j in range(16):
        place = jnp.where(codes[:, j : j + 1] == offset, refs[:, j : j + 1], place)
    coarse_idx_ref[...] = place.astype(jnp.int32) * 32

    blocks = pool_ref.reshape(145 * 128, 128)

    for level in range(2):
        copies[level].wait()
        apply_level(
            level,
            blocks,
            lambda b, code: idx_ref[(level * SLOT + b) * CODES + code],
            xbd_ref,
            yw_ref,
            zw_ref,
            spread_ref,
            table_ref,
            acc_ref,
        )
        for b in range(SLOT):
            rows = jnp.where(b < counts_ref[level, 0], acc_ref[b * K : (b + 1) * K, :], 0.0)
            if level == 0:
                out_ref[0, b] = rows.astype(BF)
            else:
                one_ref[b] = rows


def tail_kernel(
    idx_ref,
    parent_ref,
    code_ref,
    summed_ref,
    other_ref,
    one_ref,
    xbd_ref,
    yw_ref,
    zw_ref,
    filt_ref,
    fine_in_ref,
    fine_out_ref,
    coarse_out_ref,
    pool_ref,
    spread_ref,
    table_ref,
    acc_ref,
    coarse_ref,
    result_ref,
    sems,
):
    copies = []
    parity = lax.axis_index("core")
    for gp in range(4):
        for ref, side in ((summed_ref, 1 - parity), (other_ref, parity)):
            copies.append(
                pltpu.make_async_copy(
                    ref.at[:, gp], pool_ref.at[2 * gp + side], sems.at[len(copies)]
                )
            )
            copies[-1].start()
    pool_ref[8, 0:4] = jnp.zeros((4, 8, 128), BF)
    blocks = pool_ref.reshape(9 * 512, 128)
    for copy in copies:
        copy.wait()

    apply_level(
        2,
        blocks,
        lambda b, code: idx_ref[b, code],
        xbd_ref,
        yw_ref,
        zw_ref,
        spread_ref,
        table_ref,
        acc_ref,
    )
    for t in range(SLOT):
        coarse_ref[t] = acc_ref[t * K : (t + 1) * K, :]
    coarse_out_ref[0] = coarse_ref[lax.axis_index("lane")].astype(BF)

    rep_n, tile_n, _, tile_t = factors(filt_ref)
    lane_block = iota((K, KK), 1) // K
    rows = []
    for b in range(SLOT):
        chosen = jnp.where(code_ref[b] // 4 == 1, tile_t[1], tile_t[0])
        rows.append(jnp.where(lane_block == parent_ref[b], chosen, 0.0).astype(BF))
    lowered = dot(jnp.concatenate(rows, axis=0), acc_ref[...].astype(BF)).astype(BF)
    correction = dot(corner_spread(lowered, code_ref), corner_tables(rep_n, tile_n))
    for b in range(SLOT):
        result_ref[b] = (one_ref[b] + correction[b * K : (b + 1) * K, :]).astype(BF)
    copy = pltpu.make_async_copy(result_ref, fine_out_ref.at[1], sems.at[8])
    copy.start()
    copy.wait()


def smem():
    return pl.BlockSpec(memory_space=pltpu.SMEM)


def vmem():
    return pl.BlockSpec(memory_space=pltpu.VMEM)


def room(mib):
    return pltpu.CompilerParams(vmem_limit_bytes=mib * 1024 * 1024)


def anywhere():
    return pl.BlockSpec(memory_space=pl.ANY)


def code_index(codes, mask, places, empty):
    hits = (codes[:, None, :] == jnp.arange(CODES, dtype=jnp.int32)[None, :, None]) & (
        mask[:, None, :] == 1
    )
    return empty + jnp.sum(jnp.where(hits, places[:, None, :] - empty, 0), axis=2)


def body(
    fine_in,
    counts,
    neighbour_refs,
    offset_codes,
    neighbour_mask,
    send_slots,
    parent_of,
    child_code,
    coarse_refs,
    coarse_codes,
    coarse_mask,
    ops_x,
    ops_y,
    ops_z,
    filters,
):
    send = pl.pallas_call(
        send_kernel,
        in_specs=[smem()] * 3 + [vmem()] * 5,
        out_specs=anywhere(),
        out_shape=jax.ShapeDtypeStruct((128, 136, 128), BF),
        scratch_shapes=[
            pltpu.VMEM((128, 128, 128), BF),
            pltpu.VMEM((128, 8, 128), BF),
            pltpu.VMEM((SLOT + 1, K, KK), F32),
            pltpu.SemaphoreType.DMA((9,)),
        ],
        name="send",
    )(
        parent_of,
        child_code,
        send_slots,
        fine_in,
        filters,
        coarse_refs,
        coarse_codes,
        coarse_mask,
    )
    arrived = lax.all_to_all(send, AXES, split_axis=0, concat_axis=0, tiled=True)

    summed, info = pl.pallas_call(
        place_kernel,
        in_specs=[anywhere()],
        out_specs=[anywhere(), vmem()],
        out_shape=[
            jax.ShapeDtypeStruct((64, 32, 128), BF),
            jax.ShapeDtypeStruct((16, 8, 128), BF),
        ],
        scratch_shapes=[
            pltpu.VMEM((4, 16, 8, 128), BF),
            pltpu.VMEM((16, 32, 128), BF),
            pltpu.SemaphoreType.DMA((6,)),
        ],
        compiler_params=room(8),
        name="place",
    )(arrived.reshape(4, 2, 16, 136, 128))
    summed = lax.all_to_all(summed, ("lane", "y"), split_axis=0, concat_axis=0, tiled=True)

    repeat, tiled = spreads()
    yw = jnp.einsum("lmcpr,pk->lmcrk", ops_y, repeat, preferred_element_type=F32)
    zw = jnp.einsum("lmcqs,qk->lmcsk", ops_z, tiled, preferred_element_type=F32)
    yw = yw.reshape(3, 12, K, KK)
    zw = zw.reshape(3, 12, K, KK)
    xm = jnp.transpose(ops_x, (0, 1, 3, 2, 4)).reshape(3, 64, 48)
    size = GROUP * K
    row, col = iota((4 * size, 64), 0), iota((4 * size, 64), 1)
    grow = ((row // size == col // K) & (row % K == col % K)).astype(BF)
    row, col = iota((48, 3 * size), 0), iota((48, 3 * size), 1)
    wide = (col % 48 == row).astype(BF)
    row, col = iota((4 * size, 3 * size), 0), iota((4 * size, 3 * size), 1)
    own = (row % size) // K == col // 48
    xbd = jnp.einsum("ij,ljk->lik", grow, xm)
    xbd = jnp.einsum("lik,kn->lin", xbd, wide)
    xbd = jnp.where(own[None], xbd, jnp.zeros_like(xbd))

    empty = 144 * 128
    tables = []
    for level in range(2):
        refs = neighbour_refs[level]
        far = refs - SLOT
        places = jnp.where(
            refs < SLOT,
            (128 + refs) * 128 + level * 64,
            (far // CAP) * 128 + level * 64 + (far % CAP) * 32,
        )
        tables.append(code_index(offset_codes[level], neighbour_mask[level], places, empty))
    idx = jnp.concatenate([t.reshape(-1) for t in tables])
    work = [
        pltpu.VMEM((2, KK, TERMS * KK), BF),
        pltpu.VMEM((2, TERMS * KK, KK), BF),
        pltpu.VMEM((KK, KK), F32),
    ]
    fine_out, one, coarse_idx = pl.pallas_call(
        fine_kernel,
        in_specs=[smem()] * 2 + [anywhere()] + [vmem()] * 5,
        out_specs=[pl.BlockSpec((1, SLOT, K, KK), lambda i: (0, 0, 0, 0)), vmem(), vmem()],
        out_shape=[
            jax.ShapeDtypeStruct((2, SLOT, K, KK), BF),
            jax.ShapeDtypeStruct((SLOT, K, KK), F32),
            jax.ShapeDtypeStruct((16, 128), jnp.int32),
        ],
        grid=(1,),
        scratch_shapes=[pltpu.VMEM((145, 128, 128), BF)]
        + work
        + [pltpu.SemaphoreType.DMA((2,))],
        compiler_params=room(20),
        name="fine",
        cost_estimate=pl.CostEstimate(
            flops=10_000_000_000, bytes_accessed=6_000_000, transcendentals=0
        ),
    )(idx, counts, arrived, fine_in, info, xbd, yw, zw)

    summed, coarse_idx = lax.optimization_barrier((summed, coarse_idx))
    other = lax.ppermute(summed, "core", [(0, 1), (1, 0)])
    fine_out, coarse_out = pl.pallas_call(
        tail_kernel,
        in_specs=[smem()] * 3 + [anywhere()] * 2 + [vmem()] * 5 + [anywhere()],
        out_specs=[anywhere(), vmem()],
        out_shape=[
            jax.ShapeDtypeStruct((2, SLOT, K, KK), BF),
            jax.ShapeDtypeStruct((1, K, KK), BF),
        ],
        scratch_shapes=[pltpu.VMEM((9, 64, 8, 128), BF)]
        + work
        + [
            pltpu.VMEM((SLOT, K, KK), F32),
            pltpu.VMEM((SLOT, K, KK), BF),
            pltpu.SemaphoreType.DMA((9,)),
        ],
        input_output_aliases={10: 0},
        compiler_params=room(16),
        name="tail",
    )(
        coarse_idx,
        parent_of,
        child_code,
        summed.reshape(64, 4, 8, 128),
        other.reshape(64, 4, 8, 128),
        one,
        xbd,
        yw,
        zw,
        filters,
        fine_out,
    )
    return fine_out, coarse_out


def solution(mesh):
    blocks = P(None, AXES, None, None)
    table = P(None, AXES, None)
    in_specs = (
        blocks,
        P(None, AXES),
        table,
        table,
        table,
        table,
        P(AXES),
        P(AXES),
        P(AXES, None),
        P(AXES, None),
        P(AXES, None),
        P(),
        P(),
        P(),
        P(),
    )
    out_specs = (blocks, P(AXES, None, None))
    parts = (mesh.shape["grp"] // 2, 2, mesh.shape["lane"])
    mesh = jax.sharding.Mesh(mesh.devices.reshape(parts), AXES)
    return jax.shard_map(body, mesh=mesh, in_specs=in_specs, out_specs=out_specs, check_vma=False)
```
